256 devices in a mesh: dp: 2 (over core), context: 32 (over x, z), tensor: 4 (over y).
Axes of the slice: x: 4, y: 4, z: 8, core: 2. Of those that a mesh axis runs over, the one named last changes fastest.
Arguments:
- query_rows: bfloat16 [2, 8192, 4096], P('dp', 'context', 'tensor'), may hold values from -6 to 6
- key_rows: bfloat16 [2, 8192, 4096], P('dp', 'context', 'tensor'), may hold values from -6 to 6
- value_rows: bfloat16 [2, 8192, 4096], P('dp', 'context', 'tensor'), may hold values from -6 to 6
- filters: bfloat16 [256, 128], P('tensor'), may hold values from -0.5 to 0.5
- out_weight: bfloat16 [4096, 4096], P('tensor'), may hold values from -0.09375 to 0.09375
- lengths: int32 [2, 32], P('dp'), may hold values from 1 to 512, 8192 in all within a row
- panel_plan: int32 [2, 1024], P('dp'), may hold values from 0 to 1023, as said below
- out_grad: bfloat16 [2, 8192, 4096], P('dp', 'context', 'tensor'), may hold values from -6 to 6
Outputs:
- mixed: bfloat16 [2, 8192, 4096], P('dp', 'context', 'tensor')
- query_grad: bfloat16 [2, 8192, 4096], P('dp', 'context', 'tensor')
- key_grad: bfloat16 [2, 8192, 4096], P('dp', 'context', 'tensor')
- value_grad: bfloat16 [2, 8192, 4096], P('dp', 'context', 'tensor')
- filter_grad: float32 [256, 128], P('tensor')
The draws below stay inside these ranges and needn't reach their ends.
Inputs may be any that keep to these rules, and one draw needn't show every extreme that they name: Each row of panel_plan is a permutation of 0 to 1023, and within each aligned block of 32 entries (the panels of one loader index of context) the values divided by 32, rounded down, are a permutation of 0 to 31. `lengths`: each row sums to 8192.
All inputs are finite; a program needn't handle non-finite values.
Results may differ from the reference program's by a relative error of at most 0.009.
Values may be sent and summed in bfloat16 or wider, within the bound.
A program may use at most 128 MiB of HBM per device.

```python
import math
import jax
import jax.numpy as jnp
import numpy as np
from jax import lax

C_ALL = 4096
OUT = 4096
GROUP = 16
TAPS = 128
B = 2
TOKENS = 8192
PN = 32
P_SIZE = 8
NPAN = 1024
DOCS = 32
MOST = 512
N_TENSOR = 4


def draw_panel_plan(key, part):

    def one_row(row_key):
        first_key, second_key = jax.random.split(row_key)
        owner_perm = jax.vmap(lambda item: jax.random.permutation(item, PN))(jax.random.split(first_key, PN))
        slot_perm = jax.vmap(lambda item: jax.random.permutation(item, PN))(jax.random.split(second_key, PN))
        loader_ids = jnp.arange(PN, dtype=jnp.int32)[:, None]
        slot_of = slot_perm[owner_perm, loader_ids]
        return (owner_perm * PN + slot_of).reshape(PN * PN).astype(jnp.int32)
    return jax.vmap(one_row)(jax.random.split(key, B))


def steps_of(key, extent, pieces, low, largest):
    gain = 1.0
    for axis_at, shards_of in pieces:
        heights = jax.random.uniform(jax.random.fold_in(jax.random.fold_in(key, 6), axis_at), (shards_of,), jnp.float32, low / len(pieces), largest / len(pieces))
        gain = gain * jnp.repeat(jnp.exp(heights), extent[axis_at] // shards_of).reshape((-1,) + (1,) * (len(extent) - 1 - axis_at))
    return gain


def profile(amount, total, limit, lean):
    loads = [(1 << 20) // math.isqrt(standing ** lean) + 1 for standing in range(2, amount + 1)]
    spare, given = total - limit - (amount - 1), [1] * (amount - 1)
    while spare > 0:
        free = [i for i in range(amount - 1) if given[i] < limit]
        pool, remaining = sum([loads[i] for i in free]), spare
        for i in free:
            addition = min(limit - given[i], max(1, remaining * loads[i] // pool), spare)
            given[i] = given[i] + addition
            spare = spare - addition
    return np.array([limit] + given)


def ragged(key, count, total, most, skew):
    if count == 2:
        one = jax.random.randint(key, (), max(1, total - most), min(most, total - 1) + 1)
        return jnp.stack([one, total - one])
    tallies = jnp.asarray(profile(count, total, most, skew), jnp.int32)
    couples = (count - 1) // 2
    donor, sink = tallies[1:1 + 2 * couples:2], tallies[2:2 + 2 * couples:2]
    margin = jnp.minimum(donor - 1, most - sink)
    passed = jax.random.randint(jax.random.fold_in(key, 1), (couples,), 0, 1 << 20) % (margin + 1)
    tallies = tallies.at[1:1 + 2 * couples:2].set(donor - passed).at[2:2 + 2 * couples:2].set(sink + passed)
    return tallies[jax.random.permutation(jax.random.fold_in(key, 2), count)]


def noise(own_key, shape, deviation, most, cuts=(), held_as=jnp.bfloat16):
    values = jax.random.normal(own_key, shape, jnp.float32) * deviation
    if len(cuts) > 0:
        values = steps_of(own_key, shape, cuts, -0.22, 0.18) * values
    return jnp.clip(values, min=-most, max=most).astype(held_as)


def setup_inputs(seed: int = 0) -> dict:
    key_of = jax.random.split(jax.random.key(seed), 9)
    query_rows = noise(key_of[0], (B, TOKENS, C_ALL), 1.0, 6.0, ((0, 2), (1, 32), (2, 4)))
    key_rows = noise(key_of[1], (B, TOKENS, C_ALL), 1.0, 6.0, ((0, 2), (1, 32), (2, 4)))
    value_rows = noise(key_of[2], (B, TOKENS, C_ALL), 1.0, 6.0, ((0, 2), (1, 32), (2, 4)))
    filters = noise(key_of[3], (C_ALL // GROUP, TAPS), TAPS ** -0.5, 0.5, ((0, 4),))
    out_weight = noise(key_of[4], (C_ALL, OUT), C_ALL ** -0.5, 0.09375, ((0, 4),))
    lengths = jax.vmap(lambda own: ragged(own, DOCS, TOKENS, MOST, 2))(jax.random.split(key_of[5], B)).reshape((B, DOCS)).astype(jnp.int32)
    panel_plan = draw_panel_plan(jax.random.fold_in(key_of[8], 71), 0)
    out_grad = noise(key_of[7], (B, TOKENS, OUT), 1.0, 6.0, ((0, 2), (1, 32), (2, 4)))
    return dict(query_rows=query_rows, key_rows=key_rows, value_rows=value_rows, filters=filters, out_weight=out_weight, lengths=lengths, panel_plan=panel_plan, out_grad=out_grad)


def filter_forward(product, filter_cols, age):
    length, width = product.shape
    padded = jnp.concatenate([jnp.zeros((TAPS, width), jnp.float32), product.astype(jnp.float32)], axis=0)

    def step(tap, total):
        shifted = lax.dynamic_slice_in_dim(padded, (TAPS - tap).astype(jnp.int32), length, 0)
        column = lax.dynamic_slice_in_dim(filter_cols, tap.astype(jnp.int32), 1, 1)[:, 0]
        return total + jnp.where((age >= tap)[:, None], shifted * column[None, :], 0.0)
    return lax.fori_loop(0, TAPS, step, jnp.zeros((length, width), jnp.float32))

def filter_backward(conv_back, filter_cols, age):
    length, width = conv_back.shape
    padded = jnp.concatenate([conv_back.astype(jnp.float32), jnp.zeros((TAPS, width), jnp.float32)], axis=0)
    age_pad = jnp.concatenate([age, jnp.full((TAPS,), -1, jnp.int32)], axis=0)

    def step(tap, total):
        shifted = lax.dynamic_slice_in_dim(padded, tap.astype(jnp.int32), length, 0)
        later_age = lax.dynamic_slice_in_dim(age_pad, tap.astype(jnp.int32), length, 0)
        column = lax.dynamic_slice_in_dim(filter_cols, tap.astype(jnp.int32), 1, 1)[:, 0]
        return total + jnp.where((later_age >= tap)[:, None], shifted * column[None, :], 0.0)
    return lax.fori_loop(0, TAPS, step, jnp.zeros((length, width), jnp.float32))

def filter_terms(conv_back, product, age):
    length, width = product.shape
    padded = jnp.concatenate([jnp.zeros((TAPS, width), jnp.float32), product.astype(jnp.float32)], axis=0)
    back = conv_back.astype(jnp.float32)

    def one_tap(tap):
        shifted = lax.dynamic_slice_in_dim(padded, (TAPS - tap).astype(jnp.int32), length, 0)
        return lax.optimization_barrier(jnp.sum(jnp.where((age >= tap)[:, None], back * shifted, 0.0), axis=0))
    return lax.map(one_tap, jnp.arange(TAPS, dtype=jnp.int32)).T

def reference(query_rows, key_rows, value_rows, filters, out_weight, lengths, panel_plan, out_grad):
    filter_cols = jnp.repeat(filters.astype(jnp.float32), GROUP, axis=0)
    positions = jnp.arange(TOKENS, dtype=jnp.int32)
    share = C_ALL // N_TENSOR
    mixed_all, query_all, key_all, value_all = ([], [], [], [])
    filter_total = jnp.zeros((C_ALL, TAPS), jnp.float32)
    for seq in range(B):
        plan_row = panel_plan[seq].astype(jnp.int32)
        inverse = jnp.argsort(plan_row).astype(jnp.int32)

        def to_owner(rows):
            return rows.reshape(NPAN, P_SIZE, -1)[inverse].reshape(TOKENS, -1)

        def to_loader(rows):
            return rows.reshape(NPAN, P_SIZE, -1)[plan_row].reshape(TOKENS, -1)
        query_own = to_owner(query_rows[seq])
        key_own = to_owner(key_rows[seq])
        value_own = to_owner(value_rows[seq])
        product = (key_own.astype(jnp.float32) * value_own.astype(jnp.float32)).astype(jnp.bfloat16)
        starts = jnp.cumsum(lengths[seq]).astype(jnp.int32) - lengths[seq]
        begin = lax.optimization_barrier(jnp.max(jnp.where(starts[None, :] <= positions[:, None], starts[None, :], 0), axis=1))
        age = (positions - begin).astype(jnp.int32)
        conv = filter_forward(product, filter_cols, age)
        gated = (query_own.astype(jnp.float32) * conv).astype(jnp.bfloat16)
        total = jnp.zeros((TOKENS, OUT), jnp.float32)
        for part in range(N_TENSOR):
            piece = jnp.dot(gated[:, part * share:(part + 1) * share], out_weight[part * share:(part + 1) * share], preferred_element_type=jnp.float32)
            total = total + piece.astype(jnp.bfloat16).astype(jnp.float32)
        mixed_all.append(total.astype(jnp.bfloat16))
        grad_gated = jnp.dot(out_grad[seq], out_weight.T, preferred_element_type=jnp.float32)
        query_back = (grad_gated * conv).astype(jnp.bfloat16)
        conv_back = (grad_gated * query_own.astype(jnp.float32)).astype(jnp.bfloat16)
        product_back = filter_backward(conv_back, filter_cols, age).astype(jnp.bfloat16)
        key_back = (product_back.astype(jnp.float32) * value_own.astype(jnp.float32)).astype(jnp.bfloat16)
        value_back = (product_back.astype(jnp.float32) * key_own.astype(jnp.float32)).astype(jnp.bfloat16)
        filter_total = filter_total + filter_terms(conv_back, product, age)
        query_all.append(to_loader(query_back))
        key_all.append(to_loader(key_back))
        value_all.append(to_loader(value_back))
    scale = 1.0 / jnp.sqrt(jnp.float32(B * TOKENS))
    filter_grad = filter_total.reshape(C_ALL // GROUP, GROUP, TAPS).sum(axis=1) * scale
    return (jnp.stack(mixed_all), jnp.stack(query_all), jnp.stack(key_all), jnp.stack(value_all), filter_grad)
```

```python
import functools
import math

import jax
import jax.numpy as jnp
from jax import lax
from jax.experimental import pallas as pl
from jax.experimental.pallas import tpu as pltpu
from jax.sharding import Mesh
from jax.sharding import PartitionSpec as P

DP, CX, CZ, TP = "dp", "context_0", "context_1", "tensor"
CONTEXT = (CX, CZ)
BF = jnp.bfloat16
F32 = jnp.float32
I32 = jnp.int32
LANES = 128
CHUNKS = 4
MESH_ID = pl.DeviceIdType.MESH
NT = (((1,), (1,)), ((), ()))


def log2(n):
    return n.bit_length() - 1


def iota(shape, dim):
    return lax.broadcasted_iota(I32, shape, dim)


def ones_where(cond):
    return jnp.where(cond, 1.0, 0.0)


def mm(a, b):
    return jnp.dot(a, b, preferred_element_type=F32)


def mm_nt(a, b):
    return lax.dot_general(a, b, NT, preferred_element_type=F32)


def layer_kernel(
    cfg,
    plan_s, len_s, plan_v, filt_v, q_hbm, k_hbm, v_hbm, og_hbm, w_hbm,
    mixed_o, qg_o, kg_o, vg_o, fg_o,
    x1, kv, vv, w, og, fmat, hmat, pmat, rmat, sbuf, rbuf, sbuf2, rbuf2,
    qo, pw, cbw, x2, gated, gg, acc, tf, tb, mf, mb, mflip,
    rs_send, rs_recv, tap, tap1, tap2, tap3,
    ld, fs, fr, ags, agr, phs, phr, chs, chr_, bs, br, rss, rsr, t1s, t1r, t2s, t2r, t3s, t3r,
):
    n, nx, nz, ny, ndp = cfg["n"], cfg["nx"], cfg["nz"], cfg["ny"], cfg["ndp"]
    length, width, taps, docs = cfg["length"], cfg["width"], cfg["taps"], cfg["docs"]
    psz, gsz, total = length // n, 16, length * n
    cw = width // CHUNKS
    cols = cw // LANES
    blocks = length // taps
    per = LANES // gsz
    rows = per * taps
    lgn, lgp = log2(n), log2(psz)

    dp, cx, cz, ty = (lax.axis_index(a) for a in (DP, CX, CZ, TP))
    me = cx * nz + cz
    group_n = ndp * nx
    e_me = dp * nx + cx

    def ctx(index):
        return {CX: index // nz, CZ: lax.rem(index, nz)}

    def peer_e(index):
        return {DP: index // nx, CX: lax.rem(index, nx)}

    def after(k):
        return lax.rem(me + k, n)

    loads = [
        pltpu.make_async_copy(src, dst, ld.at[i])
        for i, (src, dst) in enumerate(
            [
                (k_hbm, kv),
                (v_hbm, vv),
                (q_hbm, x1.at[pl.ds(0, length)]),
                (og_hbm, og.at[ty]),
                (w_hbm, w),
            ]
        )
    ]
    for load in loads:
        load.start()

    barrier = pltpu.get_barrier_semaphore()

    @pl.loop(1, n)
    def _(k):
        pl.semaphore_signal(barrier, inc=1, device_id=ctx(after(k)), device_id_type=MESH_ID)

    for k in range(1, ny):
        pl.semaphore_signal(
            barrier, inc=1, device_id={TP: lax.rem(ty + k, ny)}, device_id_type=MESH_ID
        )
    for d in range(1, ndp):
        for k in range(nx):
            to = {DP: lax.rem(dp + d, ndp), CX: lax.rem(cx + k, nx)}
            pl.semaphore_signal(barrier, inc=1, device_id=to, device_id_type=MESH_ID)
    greeted = (n - 1) + (ny - 1) + (ndp - 1) * nx

    b = iota((8, 2 * length), 1)
    panel = (b >> lgp) & (n - 1)
    owner = jnp.zeros((8, 2 * length), I32)
    for i in range(n):
        owner = jnp.where(panel == i, plan_s[0, me * n + i] >> lgn, owner)
    target = owner * (2 * psz) + (b >> log2(length)) * psz + (b & (psz - 1))
    square = iota((2 * length, 2 * length), 0)
    fmat[...] = ones_where(square == target[0:1]).astype(BF)
    for load in loads[:3]:
        load.wait()
    x1[length : 2 * length] = (kv[...].astype(F32) * vv[...].astype(F32)).astype(BF)

    def to_blocks(value):
        return value.astype(BF).reshape(n, 2 * psz, cw)

    for c in range(CHUNKS):
        sbuf[c] = to_blocks(mm(fmat[...], x1[:, c * cw : (c + 1) * cw]))
        rbuf[c, me] = sbuf[c, me]

    pl.semaphore_wait(barrier, greeted)

    def send_blocks(src, dst, ssem, rsem):
        @pl.loop(1, n)
        def _(k):
            to = after(k)
            pltpu.make_async_remote_copy(
                src_ref=src.at[to],
                dst_ref=dst.at[me],
                send_sem=ssem,
                recv_sem=rsem,
                device_id=ctx(to),
                device_id_type=MESH_ID,
            ).start()

    def wait_bytes(ref, sem):
        pltpu.make_async_copy(ref, ref, sem).wait()

    loads[3].wait()
    ag = []
    for k in range(1, ny):
        copy = pltpu.make_async_remote_copy(
            src_ref=og.at[ty],
            dst_ref=og.at[ty],
            send_sem=ags.at[k],
            recv_sem=agr.at[k],
            device_id={TP: lax.rem(ty + k, ny)},
            device_id_type=MESH_ID,
        )
        copy.start()
        ag.append(copy)
    for c in range(CHUNKS):
        send_blocks(sbuf.at[c], rbuf.at[c], fs.at[c], fr.at[c])

    pv = plan_v[...]
    slot_of = jnp.where((pv >> lgn) == me, pv & (n - 1), 0).astype(F32)
    slot_of = jnp.broadcast_to(slot_of, (8, n * n)).astype(BF)
    gather = ones_where((iota((n * n, 2 * length), 0) >> lgn) == (iota((n * n, 2 * length), 1) >> (lgp + 1)))
    slot = mm(slot_of, gather.astype(BF)).astype(I32)
    target = ((b >> lgp) & 1) * length + slot * psz + (b & (psz - 1))
    pmat[...] = ones_where(square == target[0:1]).astype(BF)
    eye = ones_where(square == iota((2 * length, 2 * length), 1)).astype(BF)
    rmat[...] = mm_nt(eye, pmat[...]).astype(BF)
    hmat[...] = mm_nt(eye, fmat[...]).astype(BF)

    starts = []
    run = jnp.int32(0)
    for d in range(docs):
        starts.append(run)
        run = run + len_s[0, d]

    def documents(positions):
        count = jnp.zeros(positions.shape, I32)
        for start in starts:
            count = count + jnp.where(positions >= start, 1, 0)
        return jnp.where(positions >= total, docs + 1, count)

    base = me * length
    row = iota((taps, LANES), 0)
    lane = iota((taps, LANES), 1)
    lane8 = iota((8, (blocks + 2) * taps), 1)
    along = documents(base - taps + lane8)

    def same(doc_rows, first):
        return doc_rows == along[0:1, first : first + taps]

    for k in range(blocks):
        here = documents(base + k * taps + row)
        at = (k + 1) * taps
        mf[k, :, 0:taps] = ones_where(same(here, at - taps) & (lane > row))
        mf[k, :, taps : 2 * taps] = ones_where(same(here, at) & (lane <= row))
        mb[k, :, 0:taps] = ones_where(same(here, at) & (lane >= row))
        mb[k, :, taps : 2 * taps] = ones_where(same(here, at + taps) & (lane < row))
        back = taps - 1 - row
        here = documents(base + k * taps + back)
        mflip[k, :, 0:taps] = ones_where(same(here, at) & (lane >= back))
        mflip[k, :, taps : 2 * taps] = ones_where(same(here, at + taps) & (lane < back))

    filt = filt_v[...]
    turn = ones_where(((taps - row) & (taps - 1)) == lane).astype(BF)
    tap3[0] = filt.astype(F32)
    tap3[1] = mm(filt, turn)

    @pl.loop(0, cfg["groups"])
    def _(g):
        for t_ref, m_ref, which in ((tf, mf, 1), (tb, mb, 0)):
            taps_row = jnp.broadcast_to(tap3[which, pl.ds(g, 1), :], (taps, taps))
            circ = pltpu.roll(taps_row, 0, 1, stride=1, stride_axis=0)
            at = pl.ds(pl.multiple_of(g * taps, taps), taps)
            for k in range(blocks):
                t_ref[k, at, 0:taps] = (circ * m_ref[k, :, 0:taps]).astype(BF)
                t_ref[k, at, taps : 2 * taps] = (circ * m_ref[k, :, taps : 2 * taps]).astype(BF)

    loads[4].wait()

    def add_grad(source, first):
        @pl.loop(0, CHUNKS)
        def _(c):
            part = mm_nt(
                og[source],
                w[pl.ds(pl.multiple_of(c * cw, cw), cw), pl.ds(pl.multiple_of(source * width, width), width)],
            )
            gg[c] = part if first else gg[c] + part

    add_grad(ty, True)
    for k in range(1, ny):
        ag[k - 1].wait_recv()
        add_grad(lax.rem(ty - k + ny, ny), False)

    nxt, prv = ctx(after(1)), ctx(after(n - 1))
    halos = []

    def stage_a(c):
        wait_bytes(rbuf.at[c, pl.ds(0, n - 1)], fr.at[c])
        owned = mm(pmat[...], rbuf[c].reshape(2 * length, cw))
        query = owned[0:length]
        qo[c] = query.astype(BF)
        pw[c, taps : taps + length] = owned[length : 2 * length].astype(BF)
        cbw[c, 0:length] = (gg[c] * query).astype(BF)
        one = pltpu.make_async_remote_copy(
            src_ref=pw.at[c, pl.ds(length, taps)],
            dst_ref=pw.at[c, pl.ds(0, taps)],
            send_sem=phs.at[c],
            recv_sem=phr.at[c],
            device_id=nxt,
            device_id_type=MESH_ID,
        )
        two = pltpu.make_async_remote_copy(
            src_ref=cbw.at[c, pl.ds(0, taps)],
            dst_ref=cbw.at[c, pl.ds(length, taps)],
            send_sem=chs.at[c],
            recv_sem=chr_.at[c],
            device_id=prv,
            device_id_type=MESH_ID,
        )
        one.start()
        two.start()
        halos.append((one, two))

    group = lane >> log2(gsz)
    anti = ones_where(lane == taps - 1 - row).astype(BF)

    def pick(res):
        out = res[0:taps]
        for g in range(1, per):
            out = jnp.where(group == g, res[g * taps : (g + 1) * taps], out)
        return out

    def stage_b(c):
        for halo in halos[c]:
            halo.wait_recv()
        for j in range(cols):
            lanes = slice(j * LANES, (j + 1) * LANES)
            col = c * cols + j
            outer = [None] * per
            for k in range(blocks):
                own = slice(k * taps, (k + 1) * taps)
                win = slice(k * taps, (k + 2) * taps)
                t_rows = slice(col * rows, (col + 1) * rows)
                conv = pick(mm(tf[k, t_rows, :], pw[c, win, lanes]))
                gated[own, c * cw + j * LANES : c * cw + (j + 1) * LANES] = (
                    qo[c, own, lanes].astype(F32) * conv
                ).astype(BF)
                x2[c, own, lanes] = (gg[c, own, lanes] * conv).astype(BF)
                x2[c, length + k * taps : length + (k + 1) * taps, lanes] = pick(
                    mm(tb[k, t_rows, :], cbw[c, win, lanes])
                ).astype(BF)
                flipped = mm(anti, pw[c, (k + 1) * taps : (k + 2) * taps, lanes])
                stacked = jnp.concatenate(
                    [jnp.where(group == g, flipped, 0.0).astype(BF) for g in range(per)], axis=0
                )
                res = mm_nt(stacked, cbw[c, win, lanes])
                for g in range(per):
                    part = res[g * taps : (g + 1) * taps]
                    term = part[:, 0:taps] * mflip[k, :, 0:taps] + part[:, taps:] * mflip[k, :, taps:]
                    outer[g] = term if k == 0 else outer[g] + term
            tap[col] = jnp.concatenate(
                [
                    jnp.sum(pltpu.roll(o, 1, 1, stride=1, stride_axis=0), axis=0, keepdims=True)
                    for o in outer
                ],
                axis=0,
            )
        sbuf2[c] = to_blocks(mm(rmat[...], x2[c]))
        rbuf2[c, me] = sbuf2[c, me]
        send_blocks(sbuf2.at[c], rbuf2.at[c], bs.at[c], br.at[c])

        @pl.loop(0, ny)
        def _(y):
            at = pl.ds(pl.multiple_of(y * width, width), width)
            part = mm(gated[:, c * cw : (c + 1) * cw], w[c * cw : (c + 1) * cw, at])
            acc[y] = part if c == 0 else acc[y] + part

    for c in range(CHUNKS):
        stage_a(c)
    for c in range(CHUNKS):
        stage_b(c)

    rs = []
    for k in range(1, ny):
        to = lax.rem(ty + k, ny)
        rs_send[k] = acc[to].astype(BF)
        copy = pltpu.make_async_remote_copy(
            src_ref=rs_send.at[k],
            dst_ref=rs_recv.at[ty],
            send_sem=rss.at[k],
            recv_sem=rsr.at[k],
            device_id={TP: to},
            device_id_type=MESH_ID,
        )
        copy.start()
        rs.append(copy)
    rs_recv[ty] = acc[ty].astype(BF)

    firsts = []
    for k in range(1, group_n):
        to = lax.rem(e_me + k, group_n)
        copy = pltpu.make_async_remote_copy(
            src_ref=tap.at[to],
            dst_ref=tap1.at[e_me],
            send_sem=t1s.at[k],
            recv_sem=t1r.at[k],
            device_id=peer_e(to),
            device_id_type=MESH_ID,
        )
        copy.start()
        firsts.append(copy)
    tap1[e_me] = tap[e_me]
    for copy in firsts:
        copy.wait_recv()
    tap2[cz] = jnp.sum(tap1[...], axis=0)
    seconds = []
    for k in range(1, nz):
        copy = pltpu.make_async_remote_copy(
            src_ref=tap2.at[cz],
            dst_ref=tap2.at[cz],
            send_sem=t2s.at[k],
            recv_sem=t2r.at[k],
            device_id={CZ: lax.rem(cz + k, nz)},
            device_id_type=MESH_ID,
        )
        copy.start()
        seconds.append(copy)
    for copy in seconds:
        copy.wait_recv()
    summed = tap2[0]
    for z in range(1, nz):
        summed = summed + tap2[z]
    scale = 1.0 / math.sqrt(float(ndp * total))
    fg_o[e_me] = summed * scale
    thirds = []
    for k in range(1, group_n):
        copy = pltpu.make_async_remote_copy(
            src_ref=fg_o.at[e_me],
            dst_ref=fg_o.at[e_me],
            send_sem=t3s.at[k],
            recv_sem=t3r.at[k],
            device_id=peer_e(lax.rem(e_me + k, group_n)),
            device_id_type=MESH_ID,
        )
        copy.start()
        thirds.append(copy)

    for c in range(CHUNKS):
        wait_bytes(rbuf2.at[c, pl.ds(0, n - 1)], br.at[c])
        home = mm(hmat[...], rbuf2[c].reshape(2 * length, cw))
        at = slice(c * cw, (c + 1) * cw)
        qg_o[:, at] = home[0:length].astype(BF)
        kg_o[:, at] = (home[length:] * vv[:, at].astype(F32)).astype(BF)
        vg_o[:, at] = (home[length:] * kv[:, at].astype(F32)).astype(BF)
    for copy in rs:
        copy.wait_recv()
    summed = rs_recv[0].astype(F32)
    for y in range(1, ny):
        summed = summed + rs_recv[y].astype(F32)
    mixed_o[...] = summed.astype(BF)
    for copy in thirds:
        copy.wait_recv()

    for copy in ag + rs + firsts + seconds + thirds:
        copy.wait_send()
    for one, two in halos:
        one.wait_send()
        two.wait_send()
    for c in range(CHUNKS):
        wait_bytes(sbuf.at[c, pl.ds(0, n - 1)], fs.at[c])
        wait_bytes(sbuf2.at[c, pl.ds(0, n - 1)], bs.at[c])


def build(mesh, nx, nz):
    ndp, ny = mesh.shape["dp"], mesh.shape["tensor"]
    n = nx * nz
    finer = Mesh(mesh.devices.reshape(ndp, nx, nz, ny), (DP, CX, CZ, TP))

    def per_device(query, key, value, filters, weight, lengths, plan, out_grad):
        length, width = query.shape[1:]
        groups, taps = filters.shape
        cfg = dict(
            n=n, nx=nx, nz=nz, ny=ny, ndp=ndp, length=length, width=width, taps=taps,
            docs=lengths.shape[1], groups=groups,
        )
        cw, blocks, psz = width // CHUNKS, length // taps, length // n
        vmem = pl.BlockSpec(memory_space=pltpu.VMEM)
        smem = pl.BlockSpec(memory_space=pltpu.SMEM)
        hbm = pl.BlockSpec(memory_space=pl.ANY)
        dma = pltpu.SemaphoreType.DMA
        row = jax.ShapeDtypeStruct((length, width), BF)
        e = ndp * nx
        assert groups == e * 8
        outs = pl.pallas_call(
            functools.partial(layer_kernel, cfg),
            name="layer",
            out_shape=(row, row, row, row, jax.ShapeDtypeStruct((e, 8, taps), F32)),
            in_specs=[smem, smem, vmem, vmem, hbm, hbm, hbm, hbm, hbm],
            out_specs=(vmem,) * 5,
            scratch_shapes=[
                pltpu.VMEM((2 * length, width), BF),
                pltpu.VMEM((length, width), BF),
                pltpu.VMEM((length, width), BF),
                pltpu.VMEM(weight.shape, BF),
                pltpu.VMEM((ny, length, width), BF),
                *[pltpu.VMEM((2 * length, 2 * length), BF)] * 4,
                *[pltpu.VMEM((CHUNKS, n, 2 * psz, cw), BF)] * 4,
                pltpu.VMEM((CHUNKS, length, cw), BF),
                *[pltpu.VMEM((CHUNKS, length + taps, cw), BF)] * 2,
                pltpu.VMEM((CHUNKS, 2 * length, cw), BF),
                pltpu.VMEM((length, width), BF),
                pltpu.VMEM((CHUNKS, length, cw), F32),
                pltpu.VMEM((ny, length, width), F32),
                *[pltpu.VMEM((blocks, groups * taps, 2 * taps), BF)] * 2,
                *[pltpu.VMEM((blocks, taps, 2 * taps), F32)] * 3,
                *[pltpu.VMEM((ny, length, width), BF)] * 2,
                *[pltpu.VMEM((e, 8, taps), F32)] * 2,
                pltpu.VMEM((nz, 8, taps), F32),
                pltpu.VMEM((2, groups, taps), F32),
                dma((5,)),
                dma((CHUNKS,)), dma((CHUNKS,)),
                dma((ny,)), dma((ny,)),
                *[dma((CHUNKS,))] * 4,
                dma((CHUNKS,)), dma((CHUNKS,)),
                dma((ny,)), dma((ny,)),
                dma((e,)), dma((e,)),
                dma((nz,)), dma((nz,)),
                dma((e,)), dma((e,)),
            ],
            compiler_params=pltpu.CompilerParams(
                collective_id=0, has_side_effects=True, vmem_limit_bytes=67043328
            ),
        )(plan, lengths, plan, filters, query[0], key[0], value[0], out_grad[0], weight)
        mixed, qg, kg, vg, fg = outs
        return mixed[None], qg[None], kg[None], vg[None], fg.reshape(groups, taps)

    rows = P(DP, CONTEXT, TP)
    split = P(TP, None)
    return jax.shard_map(
        per_device,
        mesh=finer,
        in_specs=(rows, rows, rows, split, split, P(DP, None), P(DP, None), rows),
        out_specs=(rows, rows, rows, rows, split),
        check_vma=False,
    )


def solution(mesh):
    return build(mesh, 4, mesh.shape["context"] // 4)
```

```python
import contextlib
import functools
import math

import jax
import jax.numpy as jnp
from jax import lax
from jax.experimental import pallas as pl
from jax.experimental.pallas import tpu as pltpu
from jax.sharding import Mesh
from jax.sharding import PartitionSpec as P

DP, CX, CZ, TP = "dp", "context_0", "context_1", "tensor"
CONTEXT = (CX, CZ)
BF = jnp.bfloat16
F32 = jnp.float32
I32 = jnp.int32
LANES = 128
HALVES = 2
UNITS = 4
MESH_ID = pl.DeviceIdType.MESH
NT = (((1,), (1,)), ((), ()))


def mark(name):
    return contextlib.nullcontext()


def log2(n):
    return n.bit_length() - 1


def iota(shape, dim):
    return lax.broadcasted_iota(I32, shape, dim)


def ones_where(cond):
    return jnp.where(cond, 1.0, 0.0)


def mm(a, b):
    return jnp.dot(a, b, preferred_element_type=F32)


def mm_nt(a, b):
    return lax.dot_general(a, b, NT, preferred_element_type=F32)


def layer_kernel(
    cfg,
    plan_hbm, len_hbm, filt_hbm, q_hbm, k_hbm, v_hbm, og_hbm, w_hbm,
    mixed_h, qg_h, kg_h, vg_h, fg_h,
    plan_s, len_s, plan_v, filt_v, mixed_o, qg_o, kg_o, vg_o, fg_o,
    xp, xq, kv, vv, w, og, fmat, hmat, pmat, rmat, sbuf, rbuf, sbuf2, rbuf2,
    qo, pw, cbw, x2, gated, conv, gg, acc, tf, tb, mf, mb, mflip,
    rs_send, rs_recv, tap, tap1, tap2, tap3,
    small, out_sem, ld, fs, fr, ags, agr, phs, phr, chs, chr_, bs, br, rss, rsr, t1s, t1r, t2s, t2r, t3s, t3r,
):
    n, nx, nz, ny, ndp = cfg["n"], cfg["nx"], cfg["nz"], cfg["ny"], cfg["ndp"]
    length, width, taps, docs = cfg["length"], cfg["width"], cfg["taps"], cfg["docs"]
    psz, gsz, total = length // n, 16, length * n
    hw = width // HALVES
    uw = hw // 2
    cols = hw // LANES
    blocks = length // taps
    per = LANES // gsz
    rows = per * taps
    lgn, lgp = log2(n), log2(psz)

    dp, cx, cz, ty = (lax.axis_index(a) for a in (DP, CX, CZ, TP))
    me = cx * nz + cz
    group_n = ndp * nx
    e_me = dp * nx + cx

    def ctx(index):
        return {CX: index // nz, CZ: lax.rem(index, nz)}

    def peer_e(index):
        return {DP: index // nx, CX: lax.rem(index, nx)}

    def after(k):
        return lax.rem(me + k, n)

    barrier = pltpu.get_barrier_semaphore()

    @pl.loop(1, n)
    def _(k):
        pl.semaphore_signal(barrier, inc=1, device_id=ctx(after(k)), device_id_type=MESH_ID)

    for k in range(1, ny):
        pl.semaphore_signal(
            barrier, inc=1, device_id={TP: lax.rem(ty + k, ny)}, device_id_type=MESH_ID
        )
    for d in range(1, ndp):
        for k in range(nx):
            to = {DP: lax.rem(dp + d, ndp), CX: lax.rem(cx + k, nx)}
            pl.semaphore_signal(barrier, inc=1, device_id=to, device_id_type=MESH_ID)
    greeted = (n - 1) + (ny - 1) + (ndp - 1) * nx

    moves = [(k_hbm, kv), (v_hbm, vv), (og_hbm, og.at[ty])]
    for h in range(HALVES):
        for p in range(2):
            moves.append((q_hbm.at[:, pl.ds(h * hw + p * uw, uw)], xq.at[h, pl.ds(p * length, length)]))
    moves.append((w_hbm, w))
    loads = [pltpu.make_async_copy(src, dst, ld.at[i]) for i, (src, dst) in enumerate(moves)]
    smalls = [
        pltpu.make_async_copy(src, dst, small.at[i])
        for i, (src, dst) in enumerate(
            [(plan_hbm, plan_s), (plan_hbm, plan_v), (filt_hbm, filt_v), (len_hbm, len_s)]
        )
    ]
    for load in smalls[:1] + loads[:2] + smalls[1:] + loads[2:]:
        load.start()

    smalls[0].wait()

    b = iota((8, 2 * length), 1)
    panel = (b >> lgp) & (n - 1)
    owner = jnp.zeros((8, 2 * length), I32)
    for i in range(n):
        owner = jnp.where(panel == i, plan_s[0, me * n + i] >> lgn, owner)
    target = owner * (2 * psz) + (b >> log2(length)) * psz + (b & (psz - 1))
    square = iota((2 * length, 2 * length), 0)
    fmat[...] = ones_where(square == target[0:1]).astype(BF)
    for load in loads[:2]:
        load.wait()

    def to_blocks(value):
        return value.astype(BF).reshape(n, 2 * psz, uw)

    for h in range(HALVES):
        for p in range(2):
            at = slice(h * hw + p * uw, h * hw + (p + 1) * uw)
            xp[h, p * length : (p + 1) * length] = (
                kv[:, at].astype(F32) * vv[:, at].astype(F32)
            ).astype(BF)
        sbuf[h] = to_blocks(mm(fmat[...], xp[h]))
        rbuf[h, me] = sbuf[h, me]

    with mark("barrier"):
        pl.semaphore_wait(barrier, greeted)

    def start(src, dst, ssem, rsem, to):
        copy = pltpu.make_async_remote_copy(
            src_ref=src,
            dst_ref=dst,
            send_sem=ssem,
            recv_sem=rsem,
            device_id=to,
            device_id_type=MESH_ID,
        )
        copy.start()
        return copy

    def send_blocks(src, dst, ssem, rsem):
        @pl.loop(1, n)
        def _(k):
            to = after(k)
            start(src.at[to], dst.at[me], ssem, rsem, ctx(to))

    def send_forward(u):
        with mark("send"):
            send_blocks(sbuf.at[u], rbuf.at[u], fs.at[u], fr.at[u])

    def wait_bytes(ref, sem):
        pltpu.make_async_copy(ref, ref, sem).wait()

    half = length // 2
    up, down = {TP: lax.rem(ty + 1, ny)}, {TP: lax.rem(ty + ny - 1, ny)}
    below, above = lax.rem(ty + ny - 1, ny), lax.rem(ty + 1, ny)
    across = lax.rem(ty + 2, ny)
    first, second = pl.ds(0, half), pl.ds(half, half)

    def pass_on(source, part, to, i):
        piece = og.at[source, part]
        return start(piece, piece, ags.at[i], agr.at[i], to)

    loads[2].wait()
    ag = [
        pass_on(ty, first, up, 0),
        pass_on(ty, second, down, 1),
        pass_on(ty, second, up, 2),
        pass_on(ty, first, down, 3),
    ]
    send_forward(0)
    send_forward(1)
    for h in range(HALVES):
        for load in loads[3 + 2 * h : 5 + 2 * h]:
            load.wait()
        sbuf[HALVES + h] = to_blocks(mm(fmat[...], xq[h]))
        rbuf[HALVES + h, me] = sbuf[HALVES + h, me]

    for load in smalls[1:]:
        load.wait()
    pv = plan_v[...]
    slot_of = jnp.where((pv >> lgn) == me, pv & (n - 1), 0).astype(F32)
    slot_of = jnp.broadcast_to(slot_of, (8, n * n)).astype(BF)
    table = (n * n, 2 * length)
    gather = ones_where((iota(table, 0) >> lgn) == (iota(table, 1) >> (lgp + 1)))
    slot = mm(slot_of, gather.astype(BF)).astype(I32)
    target = ((b >> lgp) & 1) * length + slot * psz + (b & (psz - 1))
    pmat[...] = ones_where(square == target[0:1]).astype(BF)

    starts = []
    run = jnp.int32(0)
    for d in range(docs):
        starts.append(run)
        run = run + len_s[0, d]

    def documents(positions):
        count = jnp.zeros(positions.shape, I32)
        for begin in starts:
            count = count + jnp.where(positions >= begin, 1, 0)
        return jnp.where(positions >= total, docs + 1, count)

    base = me * length
    row = iota((taps, LANES), 0)
    lane = iota((taps, LANES), 1)
    lane8 = iota((8, (blocks + 2) * taps), 1)
    along = documents(base - taps + lane8)

    def same(doc_rows, at):
        return doc_rows == along[0:1, at : at + taps]

    for k in range(blocks):
        here = documents(base + k * taps + row)
        at = (k + 1) * taps
        mf[k, :, 0:taps] = ones_where(same(here, at - taps) & (lane > row))
        mf[k, :, taps : 2 * taps] = ones_where(same(here, at) & (lane <= row))
        mb[k, :, 0:taps] = ones_where(same(here, at) & (lane >= row))
        mb[k, :, taps : 2 * taps] = ones_where(same(here, at + taps) & (lane < row))
        back = taps - 1 - row
        here = documents(base + k * taps + back)
        mflip[k, :, 0:taps] = ones_where(same(here, at - taps) & (lane > back))
        mflip[k, :, taps : 2 * taps] = ones_where(same(here, at) & (lane <= back))

    filt = filt_v[...]
    turn = ones_where(((taps - row) & (taps - 1)) == lane).astype(BF)
    tap3[0] = filt.astype(F32)
    tap3[1] = mm(filt, turn)

    def circulants(t_ref, m_ref, which):
        with mark("toep"):

            @pl.loop(0, cfg["groups"], step=4)
            def _(first_group):
                for i in range(4):
                    g = first_group + i
                    taps_row = jnp.broadcast_to(tap3[which, pl.ds(g, 1), :], (taps, taps))
                    circ = pltpu.roll(taps_row, 0, 1, stride=1, stride_axis=0)
                    at = pl.ds(pl.multiple_of(g * taps, taps), taps)
                    for k in range(blocks):
                        for h in range(2):
                            part = slice(h * taps, (h + 1) * taps)
                            t_ref[k, at, part] = (circ * m_ref[k, :, part]).astype(BF)

    def add_grad(source, opening):
        with mark("gg"):

            @pl.loop(0, 2 * HALVES)
            def _(c):
                part = mm_nt(
                    og[source],
                    w[
                        pl.ds(pl.multiple_of(c * uw, uw), uw),
                        pl.ds(pl.multiple_of(source * width, width), width),
                    ],
                )
                gg[c] = part if opening else gg[c] + part

    nxt, prv = ctx(after(1)), ctx(after(n - 1))
    prod_halo, back_halo = [], []

    def arrived(u):
        with mark(f"fwait{u}"):
            wait_bytes(rbuf.at[u, pl.ds(0, n - 1)], fr.at[u])
        owned = mm(pmat[...], rbuf[u].reshape(2 * length, uw)).astype(BF)
        return owned[0:length], owned[length : 2 * length]

    def receive_product(h):
        pw[h, taps : taps + length, 0:uw], pw[h, taps : taps + length, uw:hw] = arrived(h)
        prod_halo.append(
            start(pw.at[h, pl.ds(length, taps)], pw.at[h, pl.ds(0, taps)], phs.at[h], phr.at[h], nxt)
        )
        send_forward(HALVES + h)

    def receive_query(h):
        for p, part in enumerate(arrived(HALVES + h)):
            qo[2 * h + p] = part
            cbw[h, 0:length, p * uw : (p + 1) * uw] = (
                gg[2 * h + p] * part.astype(F32)
            ).astype(BF)
        back_halo.append(
            start(cbw.at[h, pl.ds(0, taps)], cbw.at[h, pl.ds(length, taps)], chs.at[h], chr_.at[h], prv)
        )

    group = lane >> log2(gsz)
    anti = ones_where(lane == taps - 1 - row).astype(BF)

    def pick(res):
        out = res[0:taps]
        for g in range(1, per):
            out = jnp.where(group == g, res[g * taps : (g + 1) * taps], out)
        return out

    def each_tile(h):
        for j in range(cols):
            lanes = slice(j * LANES, (j + 1) * LANES)
            col = h * cols + j
            for k in range(blocks):
                own = slice(k * taps, (k + 1) * taps)
                win = slice(k * taps, (k + 2) * taps)
                yield j, col, k, lanes, own, win, slice(col * rows, (col + 1) * rows)

    def placed(j, k):
        p, at = (j * LANES) // uw, (j * LANES) % uw
        return p, slice(p * length + k * taps, p * length + (k + 1) * taps), slice(at, at + LANES)

    def filter_forward(h):
        with mark(f"phalo{h}"):
            prod_halo[h].wait_recv()
        with mark("conv"):
            for j, col, k, lanes, own, win, t_rows in each_tile(h):
                p, _, at = placed(j, k)
                conv[2 * h + p, own, at] = pick(mm(tf[k, t_rows, :], pw[h, win, lanes]))

    def pack_back(u):
        sbuf2[u] = to_blocks(mm(rmat[...], x2[u]))
        rbuf2[u, me] = sbuf2[u, me]

    def query_back(h):
        with mark("qback"):
            for p in range(2):
                x2[h, p * length : (p + 1) * length] = (gg[2 * h + p] * conv[2 * h + p]).astype(BF)
            pack_back(h)

    def gate(h):
        for p in range(2):
            at = slice(h * hw + p * uw, h * hw + (p + 1) * uw)
            gated[:, at] = (qo[2 * h + p].astype(F32) * conv[2 * h + p]).astype(BF)

    def project(y, h):
        at = pl.ds(pl.multiple_of(y * width, width), width)
        rows_in = slice(h * hw, (h + 1) * hw)
        return mm(gated[:, rows_in], w[rows_in, at])

    def product_back(h):
        u = HALVES + h
        with mark(f"chalo{h}"):
            back_halo[h].wait_recv()
        with mark("pback"):
            for j, _, k, lanes, _, win, t_rows in each_tile(h):
                _, to, at = placed(j, k)
                x2[u, to, at] = pick(mm(tb[k, t_rows, :], cbw[h, win, lanes])).astype(BF)
            pack_back(u)

    def send_back(u):
        with mark("send2"):
            send_blocks(sbuf2.at[u], rbuf2.at[u], bs.at[u], br.at[u])

    def filter_terms(h):
        with mark("terms"):
            for _, col, k, lanes, own, win, _ in each_tile(h):
                if k == 0:
                    outer = [None] * per
                flipped = mm(anti, cbw[h, own, lanes])
                stacked = jnp.concatenate(
                    [jnp.where(group == g, flipped, 0.0).astype(BF) for g in range(per)], axis=0
                )
                res = mm_nt(stacked, pw[h, win, lanes])
                for g in range(per):
                    part = res[g * taps : (g + 1) * taps]
                    term = (
                        part[:, 0:taps] * mflip[k, :, 0:taps]
                        + part[:, taps:] * mflip[k, :, taps:]
                    )
                    outer[g] = term if k == 0 else outer[g] + term
                if k == blocks - 1:
                    turned = [pltpu.roll(o, 0, 1, stride=1, stride_axis=0) for o in outer]
                    tap[col] = jnp.concatenate(
                        [jnp.sum(o, axis=0, keepdims=True) for o in turned], axis=0
                    )

    circulants(tf, mf, 1)
    receive_product(0)
    with mark("agw"):
        ag[0].wait_recv()
        ag.append(pass_on(below, first, up, 4))
        ag[1].wait_recv()
        ag.append(pass_on(above, second, down, 5))
    eye = ones_where(square == iota((2 * length, 2 * length), 1)).astype(BF)
    rmat[...] = mm_nt(eye, pmat[...]).astype(BF)
    hmat[...] = mm_nt(eye, fmat[...]).astype(BF)
    with mark("wwait"):
        loads[-1].wait()
    add_grad(ty, True)
    receive_product(1)
    circulants(tb, mb, 0)
    filter_forward(0)
    with mark("agw2"):
        ag[2].wait_recv()
        ag[3].wait_recv()
    add_grad(below, False)
    add_grad(above, False)
    with mark("agw3"):
        ag[4].wait_recv()
        ag[5].wait_recv()
    add_grad(across, False)
    query_back(0)
    send_back(0)
    receive_query(0)
    gate(0)
    with mark("proj"):

        @pl.loop(0, ny)
        def _(y):
            acc[y] = project(y, 0)

    filter_terms(0)
    filter_forward(1)
    query_back(1)
    receive_query(1)
    gate(1)

    rs = []
    with mark("proj"):
        for k in range(1, ny):
            to = lax.rem(ty + k, ny)
            rs_send[k] = (acc[to] + project(to, 1)).astype(BF)
            rs.append(start(rs_send.at[k], rs_recv.at[ty], rss.at[k], rsr.at[k], {TP: to}))
        rs_recv[ty] = (acc[ty] + project(ty, 1)).astype(BF)

    filter_terms(1)
    firsts = []
    for k in range(1, group_n):
        to = lax.rem(e_me + k, group_n)
        firsts.append(start(tap.at[to], tap1.at[e_me], t1s.at[k], t1r.at[k], peer_e(to)))
    tap1[e_me] = tap[e_me]
    send_back(1)

    product_back(0)
    send_back(2)
    product_back(1)
    with mark("t1wait"):
        for copy in firsts:
            copy.wait_recv()
    tap2[cz] = jnp.sum(tap1[...], axis=0)
    seconds = []
    for k in range(1, nz):
        to = {CZ: lax.rem(cz + k, nz)}
        seconds.append(start(tap2.at[cz], tap2.at[cz], t2s.at[k], t2r.at[k], to))
    send_back(3)

    leaving = []

    def leave(src, dst):
        copy = pltpu.make_async_copy(src, dst, out_sem.at[len(leaving)])
        copy.start()
        leaving.append(copy)

    def loader_rows(u):
        h = u % HALVES
        with mark(f"bwait{u}"):
            wait_bytes(rbuf2.at[u, pl.ds(0, n - 1)], br.at[u])
        home = mm(hmat[...], rbuf2[u].reshape(2 * length, uw))
        for p in range(2):
            part = home[p * length : (p + 1) * length]
            at = slice(h * hw + p * uw, h * hw + (p + 1) * uw)
            if u < HALVES:
                qg_o[:, at] = part.astype(BF)
            else:
                kg_o[:, at] = (part * vv[:, at].astype(F32)).astype(BF)
                vg_o[:, at] = (part * kv[:, at].astype(F32)).astype(BF)
        at = pl.ds(h * hw, hw)
        for held, out in [(qg_o, qg_h)] if u < HALVES else [(kg_o, kg_h), (vg_o, vg_h)]:
            leave(held.at[:, at], out.at[:, at])

    loader_rows(0)
    loader_rows(1)
    with mark("t2wait"):
        for copy in seconds:
            copy.wait_recv()
    summed = tap2[0]
    for z in range(1, nz):
        summed = summed + tap2[z]
    scale = 1.0 / math.sqrt(float(ndp * total))
    mirror = ones_where(lane == taps - 1 - row)
    fg_o[e_me] = scale * jnp.dot(
        summed, mirror, precision=lax.Precision.HIGHEST, preferred_element_type=F32
    )
    thirds = []
    for k in range(1, group_n):
        to = peer_e(lax.rem(e_me + k, group_n))
        thirds.append(start(fg_o.at[e_me], fg_o.at[e_me], t3s.at[k], t3r.at[k], to))
    loader_rows(2)
    with mark("rswait"):
        for copy in rs:
            copy.wait_recv()
    summed = rs_recv[0].astype(F32)
    for y in range(1, ny):
        summed = summed + rs_recv[y].astype(F32)
    mixed_o[...] = summed.astype(BF)
    leave(mixed_o, mixed_h)
    with mark("t3wait"):
        for copy in thirds:
            copy.wait_recv()
    leave(fg_o, fg_h)
    loader_rows(3)

    with mark("drain"):
        for copy in ag + rs + prod_halo + back_halo + firsts + seconds + thirds:
            copy.wait_send()
        for u in range(UNITS):
            wait_bytes(sbuf.at[u, pl.ds(0, n - 1)], fs.at[u])
            wait_bytes(sbuf2.at[u, pl.ds(0, n - 1)], bs.at[u])
        for copy in leaving:
            copy.wait()


def hand_over(*refs):
    count = (len(refs) - 2) // 3
    srcs, dsts, held = refs[:count], refs[count : 2 * count], refs[2 * count : 3 * count]
    sem_in, sem_out = refs[3 * count :]
    ins = [pltpu.make_async_copy(a, b, sem_in.at[i]) for i, (a, b) in enumerate(zip(srcs, held, strict=True))]
    outs = [pltpu.make_async_copy(b, a, sem_out.at[i]) for i, (a, b) in enumerate(zip(dsts, held, strict=True))]
    for copy in ins:
        copy.start()
    for arrive, leave in zip(ins, outs, strict=True):
        arrive.wait()
        leave.start()
    for copy in outs:
        copy.wait()


def build(mesh, nx, nz):
    ndp, ny = mesh.shape["dp"], mesh.shape["tensor"]
    n = nx * nz
    finer = Mesh(mesh.devices.reshape(ndp, nx, nz, ny), (DP, CX, CZ, TP))

    def per_device(query, key, value, filters, weight, lengths, plan, out_grad):
        length, width = query.shape[1:]
        groups, taps = filters.shape
        cfg = dict(
            n=n, nx=nx, nz=nz, ny=ny, ndp=ndp, length=length, width=width, taps=taps,
            docs=lengths.shape[1], groups=groups,
        )
        hw, blocks, psz = width // HALVES, length // taps, length // n
        uw = hw // 2
        hbm = pl.BlockSpec(memory_space=pl.ANY)
        dma = pltpu.SemaphoreType.DMA
        row = jax.ShapeDtypeStruct((length, width), BF)
        e = ndp * nx
        assert groups == e * 8
        outs = pl.pallas_call(
            functools.partial(layer_kernel, cfg),
            name="layer",
            out_shape=[row, row, row, row, jax.ShapeDtypeStruct((e, 8, taps), F32)],
            in_specs=[hbm] * 8,
            out_specs=[hbm] * 5,
            scratch_shapes=[
                pltpu.SMEM(plan.shape, I32),
                pltpu.SMEM(lengths.shape, I32),
                pltpu.VMEM(plan.shape, I32),
                pltpu.VMEM(filters.shape, BF),
                *[pltpu.VMEM((length, width), BF)] * 4,
                pltpu.VMEM((e, 8, taps), F32),
                *[pltpu.VMEM((HALVES, 2 * length, uw), BF)] * 2,
                pltpu.VMEM((length, width), BF),
                pltpu.VMEM((length, width), BF),
                pltpu.VMEM(weight.shape, BF),
                pltpu.VMEM((ny, length, width), BF),
                *[pltpu.VMEM((2 * length, 2 * length), BF)] * 4,
                *[pltpu.VMEM((UNITS, n, 2 * psz, uw), BF)] * 4,
                pltpu.VMEM((2 * HALVES, length, uw), BF),
                *[pltpu.VMEM((HALVES, length + taps, hw), BF)] * 2,
                pltpu.VMEM((UNITS, 2 * length, uw), BF),
                pltpu.VMEM((length, width), BF),
                *[pltpu.VMEM((2 * HALVES, length, uw), F32)] * 2,
                pltpu.VMEM((ny, length, width), F32),
                *[pltpu.VMEM((blocks, groups * taps, 2 * taps), BF)] * 2,
                *[pltpu.VMEM((blocks, taps, 2 * taps), F32)] * 3,
                *[pltpu.VMEM((ny, length, width), BF)] * 2,
                *[pltpu.VMEM((e, 8, taps), F32)] * 2,
                pltpu.VMEM((nz, 8, taps), F32),
                pltpu.VMEM((2, groups, taps), F32),
                dma((4,)), dma((8,)), dma((8,)),
                dma((UNITS,)), dma((UNITS,)),
                dma((6,)), dma((6,)),
                *[dma((HALVES,))] * 4,
                dma((UNITS,)), dma((UNITS,)),
                dma((ny,)), dma((ny,)),
                dma((e,)), dma((e,)),
                dma((nz,)), dma((nz,)),
                dma((e,)), dma((e,)),
            ],
            compiler_params=pltpu.CompilerParams(
                collective_id=0, has_side_effects=True, vmem_limit_bytes=67043328
            ),
        )(plan, lengths, filters, query[0], key[0], value[0], out_grad[0], weight)
        moved = pl.pallas_call(
            hand_over,
            name="results",
            out_shape=[jax.ShapeDtypeStruct(o.shape, o.dtype) for o in outs],
            in_specs=[hbm] * 5,
            out_specs=[hbm] * 5,
            scratch_shapes=[pltpu.VMEM(o.shape, o.dtype) for o in outs] + [dma((5,)), dma((5,))],
        )(*outs)
        mixed, qg, kg, vg, fg = moved
        return mixed[None], qg[None], kg[None], vg[None], fg.reshape(groups, taps)

    rows = P(DP, CONTEXT, TP)
    split = P(TP, None)
    return jax.shard_map(
        per_device,
        mesh=finer,
        in_specs=(rows, rows, rows, split, split, P(DP, None), P(DP, None), rows),
        out_specs=(rows, rows, rows, rows, split),
        check_vma=False,
    )


def solution(mesh):
    return build(mesh, 4, mesh.shape["context"] // 4)
```

```python
import contextlib
import functools
import math

import jax
import jax.numpy as jnp
from jax import lax
from jax.experimental import pallas as pl
from jax.experimental.pallas import tpu as pltpu
from jax.sharding import Mesh
from jax.sharding import PartitionSpec as P

DP, CX, CZ, TP = "dp", "context_0", "context_1", "tensor"
CONTEXT = (CX, CZ)
BF = jnp.bfloat16
F32 = jnp.float32
I32 = jnp.int32
LANES = 128
HALVES = 2
UNITS = 4
MESH_ID = pl.DeviceIdType.MESH
NT = (((1,), (1,)), ((), ()))


def mark(name):
    return contextlib.nullcontext()


def log2(n):
    return n.bit_length() - 1


def iota(shape, dim):
    return lax.broadcasted_iota(I32, shape, dim)


def ones_where(cond):
    return jnp.where(cond, 1.0, 0.0)


def mm(a, b):
    return jnp.dot(a, b, preferred_element_type=F32)


def mm_nt(a, b):
    return lax.dot_general(a, b, NT, preferred_element_type=F32)


def layer_kernel(
    cfg,
    plan_hbm, len_hbm, filt_hbm, q_hbm, k_hbm, v_hbm, og_hbm, w_hbm,
    mixed_h, qg_h, kg_h, vg_h, fg_h,
    plan_s, len_s, plan_v, filt_v, mixed_o, qg_o, kg_o, vg_o, fg_o,
    xp, xq, kv, vv, w, og, fmat, hmat, pmat, rmat, sbuf, rbuf, sbuf2, rbuf2,
    qo, pw, cbw, x2, gated, conv, gg, acc, tf, tb, mf, mb, mflip,
    rs_send, rs_mid, rs_fin, tap, tap1, tap2, tap3,
    small, out_sem, ld, fs, fr, ags, agr, phs, phr, chs, chr_, bs, br, rss, rsr, t1s, t1r, t2s, t2r, t3s, t3r,
):
    n, nx, nz, ny, ndp = cfg["n"], cfg["nx"], cfg["nz"], cfg["ny"], cfg["ndp"]
    length, width, taps, docs = cfg["length"], cfg["width"], cfg["taps"], cfg["docs"]
    psz, gsz, total = length // n, 16, length * n
    hw = width // HALVES
    uw = hw // 2
    cols = hw // LANES
    blocks = length // taps
    per = LANES // gsz
    rows = per * taps
    lgn, lgp = log2(n), log2(psz)

    dp, cx, cz, ty = (lax.axis_index(a) for a in (DP, CX, CZ, TP))
    me = cx * nz + cz
    group_n = ndp * nx
    e_me = dp * nx + cx

    def ctx(index):
        return {CX: index // nz, CZ: lax.rem(index, nz)}

    def peer_e(index):
        return {DP: index // nx, CX: lax.rem(index, nx)}

    def after(k):
        return lax.rem(me + k, n)

    moves = [(k_hbm, kv), (v_hbm, vv), (og_hbm, og.at[ty])]
    for h in range(HALVES):
        for p in range(2):
            moves.append((q_hbm.at[:, pl.ds(h * hw + p * uw, uw)], xq.at[h, pl.ds(p * length, length)]))
    moves.append((w_hbm, w))
    loads = [pltpu.make_async_copy(src, dst, ld.at[i]) for i, (src, dst) in enumerate(moves)]
    small_moves = [(plan_hbm, plan_s), (plan_hbm, plan_v), (filt_hbm, filt_v), (len_hbm, len_s)]
    smalls = [
        pltpu.make_async_copy(src, dst, small.at[i]) for i, (src, dst) in enumerate(small_moves)
    ]
    smalls[0].start()

    barrier = pltpu.get_barrier_semaphore()

    def greet(to):
        pl.semaphore_signal(barrier, inc=1, device_id=to, device_id_type=MESH_ID)

    def far_first(count):
        return sorted(range(count), key=lambda d: -min(d, count - d))

    for dx in far_first(nx):
        for dz in far_first(nz):
            if (dx, dz) != (0, 0):
                greet({CX: lax.rem(cx + dx, nx), CZ: lax.rem(cz + dz, nz)})
    for d in range(1, ndp):
        for k in far_first(nx):
            greet({DP: lax.rem(dp + d, ndp), CX: lax.rem(cx + k, nx)})
    for k in range(1, ny):
        greet({TP: lax.rem(ty + k, ny)})
    greeted = (n - 1) + (ny - 1) + (ndp - 1) * nx
    for load in loads[:2] + smalls[1:] + loads[2:]:
        load.start()

    smalls[0].wait()

    sc = mark('fbuild'); sc.__enter__()
    b = iota((8, 2 * length), 1)
    panel = (b >> lgp) & (n - 1)
    owner = jnp.zeros((8, 2 * length), I32)
    for i in range(n):
        owner = jnp.where(panel == i, plan_s[0, me * n + i] >> lgn, owner)
    target = owner * (2 * psz) + (b >> log2(length)) * psz + (b & (psz - 1))
    square = iota((2 * length, 2 * length), 0)
    fmat[...] = ones_where(square == target[0:1]).astype(BF)
    sc.__exit__(None, None, None)
    with mark('kvwait'):
        for load in loads[:2]:
            load.wait()

    def to_blocks(value):
        return value.astype(BF).reshape(n, 2 * psz, uw)

    for h in range(HALVES):
        for p in range(2):
            at = slice(h * hw + p * uw, h * hw + (p + 1) * uw)
            xp[h, p * length : (p + 1) * length] = (
                kv[:, at].astype(F32) * vv[:, at].astype(F32)
            ).astype(BF)
    def own_blocks(u, x):
        sbuf[u] = to_blocks(mm(fmat[...], x))
        rbuf[u, me] = sbuf[u, me]

    own_blocks(0, xp[0])
    with mark("barrier"):
        pl.semaphore_wait(barrier, greeted)

    def start(src, dst, ssem, rsem, to):
        copy = pltpu.make_async_remote_copy(
            src_ref=src,
            dst_ref=dst,
            send_sem=ssem,
            recv_sem=rsem,
            device_id=to,
            device_id_type=MESH_ID,
        )
        copy.start()
        return copy

    def send_blocks(src, dst, ssem, rsem):
        @pl.loop(1, n)
        def _(k):
            to = after(k)
            start(src.at[to], dst.at[me], ssem, rsem, ctx(to))

    def send_forward(u):
        with mark("send"):
            send_blocks(sbuf.at[u], rbuf.at[u], fs.at[u], fr.at[u])

    def wait_bytes(ref, sem):
        pltpu.make_async_copy(ref, ref, sem).wait()

    half = length // 2
    up, down = {TP: lax.rem(ty + 1, ny)}, {TP: lax.rem(ty + ny - 1, ny)}
    below, above = lax.rem(ty + ny - 1, ny), lax.rem(ty + 1, ny)
    across = lax.rem(ty + 2, ny)
    first, second = pl.ds(0, half), pl.ds(half, half)

    def pass_on(source, part, to, i):
        piece = og.at[source, part]
        return start(piece, piece, ags.at[i], agr.at[i], to)

    send_forward(0)
    loads[2].wait()
    ag = [
        pass_on(ty, first, up, 0),
        pass_on(ty, second, down, 1),
        pass_on(ty, second, up, 2),
        pass_on(ty, first, down, 3),
    ]
    own_blocks(1, xp[1])
    send_forward(1)
    for h in range(HALVES):
        for load in loads[3 + 2 * h : 5 + 2 * h]:
            load.wait()
        own_blocks(HALVES + h, xq[h])

    for load in smalls[1:]:
        load.wait()
    pv = plan_v[...]
    slot_of = jnp.where((pv >> lgn) == me, pv & (n - 1), 0).astype(F32)
    slot_of = jnp.broadcast_to(slot_of, (8, n * n)).astype(BF)
    table = (n * n, 2 * length)
    gather = ones_where((iota(table, 0) >> lgn) == (iota(table, 1) >> (lgp + 1)))
    slot = mm(slot_of, gather.astype(BF)).astype(I32)
    target = ((b >> lgp) & 1) * length + slot * psz + (b & (psz - 1))
    pmat[...] = ones_where(square == target[0:1]).astype(BF)

    starts = []
    run = jnp.int32(0)
    for d in range(docs):
        starts.append(run)
        run = run + len_s[0, d]

    def documents(positions):
        count = jnp.zeros(positions.shape, I32)
        for begin in starts:
            count = count + jnp.where(positions >= begin, 1, 0)
        return jnp.where(positions >= total, docs + 1, count)

    base = me * length
    row = iota((taps, LANES), 0)
    lane = iota((taps, LANES), 1)
    lane8 = iota((8, (blocks + 2) * taps), 1)
    along = documents(base - taps + lane8)

    def same(doc_rows, at):
        return doc_rows == along[0:1, at : at + taps]

    for k in range(blocks):
        here = documents(base + k * taps + row)
        at = (k + 1) * taps
        mf[k, :, 0:taps] = ones_where(same(here, at - taps) & (lane > row))
        mf[k, :, taps : 2 * taps] = ones_where(same(here, at) & (lane <= row))
        mb[k, :, 0:taps] = ones_where(same(here, at) & (lane >= row))
        mb[k, :, taps : 2 * taps] = ones_where(same(here, at + taps) & (lane < row))
        back = taps - 1 - row
        here = documents(base + k * taps + back)
        mflip[k, :, 0:taps] = ones_where(same(here, at - taps) & (lane > back))
        mflip[k, :, taps : 2 * taps] = ones_where(same(here, at) & (lane <= back))

    filt = filt_v[...]
    turn = ones_where(((taps - row) & (taps - 1)) == lane).astype(BF)
    tap3[0] = filt.astype(F32)
    tap3[1] = mm(filt, turn)

    def circulants(t_ref, m_ref, which):
        with mark("toep"):

            @pl.loop(0, cfg["groups"], step=4)
            def _(first_group):
                for i in range(4):
                    g = first_group + i
                    taps_row = jnp.broadcast_to(tap3[which, pl.ds(g, 1), :], (taps, taps))
                    circ = pltpu.roll(taps_row, 0, 1, stride=1, stride_axis=0)
                    at = pl.ds(pl.multiple_of(g * taps, taps), taps)
                    for k in range(blocks):
                        for h in range(2):
                            part = slice(h * taps, (h + 1) * taps)
                            t_ref[k, at, part] = (circ * m_ref[k, :, part]).astype(BF)

    def add_grad(source, opening):
        with mark("gg"):

            @pl.loop(0, 2 * HALVES)
            def _(c):
                part = mm_nt(
                    og[source],
                    w[
                        pl.ds(pl.multiple_of(c * uw, uw), uw),
                        pl.ds(pl.multiple_of(source * width, width), width),
                    ],
                )
                gg[c] = part if opening else gg[c] + part

    nxt, prv = ctx(after(1)), ctx(after(n - 1))
    prod_halo, back_halo = [], []

    def arrived(u):
        with mark(f"fwait{u}"):
            wait_bytes(rbuf.at[u, pl.ds(0, n - 1)], fr.at[u])
        owned = mm(pmat[...], rbuf[u].reshape(2 * length, uw)).astype(BF)
        return owned[0:length], owned[length : 2 * length]

    def receive_product(h):
        pw[h, taps : taps + length, 0:uw], pw[h, taps : taps + length, uw:hw] = arrived(h)
        prod_halo.append(
            start(pw.at[h, pl.ds(length, taps)], pw.at[h, pl.ds(0, taps)], phs.at[h], phr.at[h], nxt)
        )
        send_forward(HALVES + h)

    def receive_query(h):
        for p, part in enumerate(arrived(HALVES + h)):
            qo[2 * h + p] = part
            cbw[h, 0:length, p * uw : (p + 1) * uw] = (
                gg[2 * h + p] * part.astype(F32)
            ).astype(BF)
        back_halo.append(
            start(cbw.at[h, pl.ds(0, taps)], cbw.at[h, pl.ds(length, taps)], chs.at[h], chr_.at[h], prv)
        )

    group = lane >> log2(gsz)
    anti = ones_where(lane == taps - 1 - row).astype(BF)

    def pick(res):
        out = res[0:taps]
        for g in range(1, per):
            out = jnp.where(group == g, res[g * taps : (g + 1) * taps], out)
        return out

    def each_tile(h):
        for j in range(cols):
            lanes = slice(j * LANES, (j + 1) * LANES)
            col = h * cols + j
            for k in range(blocks):
                own = slice(k * taps, (k + 1) * taps)
                win = slice(k * taps, (k + 2) * taps)
                yield j, col, k, lanes, own, win, slice(col * rows, (col + 1) * rows)

    def placed(j, k):
        p, at = (j * LANES) // uw, (j * LANES) % uw
        return p, slice(p * length + k * taps, p * length + (k + 1) * taps), slice(at, at + LANES)

    def filter_forward(h):
        with mark(f"phalo{h}"):
            prod_halo[h].wait_recv()
        with mark("conv"):
            for j, col, k, lanes, own, win, t_rows in each_tile(h):
                p, _, at = placed(j, k)
                conv[2 * h + p, own, at] = pick(mm(tf[k, t_rows, :], pw[h, win, lanes]))

    def pack_back(u):
        sbuf2[u] = to_blocks(mm(rmat[...], x2[u]))
        rbuf2[u, me] = sbuf2[u, me]

    def query_back(h):
        with mark("qback"):
            for p in range(2):
                x2[h, p * length : (p + 1) * length] = (gg[2 * h + p] * conv[2 * h + p]).astype(BF)
            pack_back(h)

    def gate(h):
        for p in range(2):
            at = slice(h * hw + p * uw, h * hw + (p + 1) * uw)
            gated[:, at] = (qo[2 * h + p].astype(F32) * conv[2 * h + p]).astype(BF)

    def project(y, h):
        at = pl.ds(pl.multiple_of(y * width, width), width)
        rows_in = slice(h * hw, (h + 1) * hw)
        return mm(gated[:, rows_in], w[rows_in, at])

    def product_back(h):
        u = HALVES + h
        with mark(f"chalo{h}"):
            back_halo[h].wait_recv()
        with mark("pback"):
            for j, _, k, lanes, _, win, t_rows in each_tile(h):
                _, to, at = placed(j, k)
                x2[u, to, at] = pick(mm(tb[k, t_rows, :], cbw[h, win, lanes])).astype(BF)
            pack_back(u)

    def send_back(u):
        with mark("send2"):
            send_blocks(sbuf2.at[u], rbuf2.at[u], bs.at[u], br.at[u])

    def filter_terms(h):
        with mark("terms"):
            for _, col, k, lanes, own, win, _ in each_tile(h):
                if k == 0:
                    outer = [None] * per
                flipped = mm(anti, cbw[h, own, lanes])
                stacked = jnp.concatenate(
                    [jnp.where(group == g, flipped, 0.0).astype(BF) for g in range(per)], axis=0
                )
                res = mm_nt(stacked, pw[h, win, lanes])
                for g in range(per):
                    part = res[g * taps : (g + 1) * taps]
                    term = (
                        part[:, 0:taps] * mflip[k, :, 0:taps]
                        + part[:, taps:] * mflip[k, :, taps:]
                    )
                    outer[g] = term if k == 0 else outer[g] + term
                if k == blocks - 1:
                    turned = [pltpu.roll(o, 0, 1, stride=1, stride_axis=0) for o in outer]
                    tap[col] = jnp.concatenate(
                        [jnp.sum(o, axis=0, keepdims=True) for o in turned], axis=0
                    )

    circulants(tf, mf, 1)
    receive_product(0)
    with mark("agw"):
        ag[0].wait_recv()
        ag.append(pass_on(below, first, up, 4))
        ag[1].wait_recv()
        ag.append(pass_on(above, second, down, 5))
    eye = ones_where(square == iota((2 * length, 2 * length), 1)).astype(BF)
    rmat[...] = mm_nt(eye, pmat[...]).astype(BF)
    hmat[...] = mm_nt(eye, fmat[...]).astype(BF)
    with mark("wwait"):
        loads[-1].wait()
    add_grad(ty, True)
    receive_product(1)
    circulants(tb, mb, 0)
    filter_forward(0)
    with mark("agw2"):
        ag[2].wait_recv()
        ag[3].wait_recv()
    add_grad(below, False)
    add_grad(above, False)
    with mark("agw3"):
        ag[4].wait_recv()
        ag[5].wait_recv()
    add_grad(across, False)
    query_back(0)
    send_back(0)
    receive_query(0)
    gate(0)
    with mark("proj"):

        @pl.loop(0, ny)
        def _(y):
            acc[y] = project(y, 0)

    filter_terms(0)
    filter_forward(1)
    query_back(1)
    receive_query(1)
    gate(1)

    filter_terms(1)
    firsts = []
    for k in range(1, nz):
        to = lax.rem(cz + k, nz)
        firsts.append(start(tap.at[to], tap1.at[cz], t1s.at[k], t1r.at[k], {CZ: to}))
    tap1[cz] = tap[cz]
    send_back(1)

    lo, hi = slice(0, half), slice(half, length)

    def reduce_send(i, dst, to):
        return start(rs_send.at[i], dst, rss.at[i], rsr.at[i], to)

    with mark("proj"):
        part = acc[across] + project(across, 1)
        rs_send[0] = part[lo].astype(BF)
        rs_send[1] = part[hi].astype(BF)
        rs = [reduce_send(0, rs_mid.at[0], up), reduce_send(1, rs_mid.at[1], down)]
        part = acc[above] + project(above, 1)
        rs_send[2] = part[hi].astype(BF)
        rs.append(reduce_send(2, rs_fin.at[0], up))
        acc[above, lo] = part[lo]
        part = acc[below] + project(below, 1)
        rs_send[3] = part[lo].astype(BF)
        rs.append(reduce_send(3, rs_fin.at[1], down))
        acc[below, hi] = part[hi]
        acc[ty] = (acc[ty] + project(ty, 1)).astype(BF).astype(F32)

    product_back(0)
    send_back(2)
    product_back(1)
    with mark("t1wait"):
        for copy in firsts:
            copy.wait_recv()
    tap2[e_me] = jnp.sum(tap1[...], axis=0)
    seconds = []
    for k in range(1, group_n):
        to = peer_e(lax.rem(e_me + k, group_n))
        seconds.append(start(tap2.at[e_me], tap2.at[e_me], t2s.at[k], t2r.at[k], to))
    send_back(3)
    with mark("rsmid"):
        rs[0].wait_recv()
        rs_send[4] = (acc[above, lo] + rs_mid[0].astype(F32)).astype(BF)
        rs.append(reduce_send(4, rs_fin.at[2], up))
        rs[1].wait_recv()
        rs_send[5] = (acc[below, hi] + rs_mid[1].astype(F32)).astype(BF)
        rs.append(reduce_send(5, rs_fin.at[3], down))

    leaving = []

    def leave(src, dst):
        copy = pltpu.make_async_copy(src, dst, out_sem.at[len(leaving)])
        copy.start()
        leaving.append(copy)

    def loader_rows(u):
        h = u % HALVES
        with mark(f"bwait{u}"):
            wait_bytes(rbuf2.at[u, pl.ds(0, n - 1)], br.at[u])
        home = mm(hmat[...], rbuf2[u].reshape(2 * length, uw))
        for p in range(2):
            part = home[p * length : (p + 1) * length]
            at = slice(h * hw + p * uw, h * hw + (p + 1) * uw)
            if u < HALVES:
                qg_o[:, at] = part.astype(BF)
            else:
                kg_o[:, at] = (part * vv[:, at].astype(F32)).astype(BF)
                vg_o[:, at] = (part * kv[:, at].astype(F32)).astype(BF)
        at = pl.ds(h * hw, hw)
        for held, out in [(qg_o, qg_h)] if u < HALVES else [(kg_o, kg_h), (vg_o, vg_h)]:
            leave(held.at[:, at], out.at[:, at])

    loader_rows(0)
    with mark("t2wait"):
        for copy in seconds:
            copy.wait_recv()
    summed = tap2[0]
    for i in range(1, group_n):
        summed = summed + tap2[i]
    scale = 1.0 / math.sqrt(float(ndp * total))
    mirror = ones_where(lane == taps - 1 - row)
    fg_o[cz] = scale * jnp.dot(
        summed, mirror, precision=lax.Precision.HIGHEST, preferred_element_type=F32
    )
    thirds = []
    for k in range(1, nz):
        to = {CZ: lax.rem(cz + k, nz)}
        thirds.append(start(fg_o.at[cz], fg_o.at[cz], t3s.at[k], t3r.at[k], to))
    loader_rows(1)
    loader_rows(2)
    with mark("rswait"):
        for copy in rs[2:]:
            copy.wait_recv()
    for rows_of, one, two in ((lo, 1, 2), (hi, 0, 3)):
        summed = acc[ty, rows_of] + rs_fin[one].astype(F32) + rs_fin[two].astype(F32)
        mixed_o[rows_of] = summed.astype(BF)
    leave(mixed_o, mixed_h)
    loader_rows(3)
    with mark("t3wait"):
        for copy in thirds:
            copy.wait_recv()
    leave(fg_o, fg_h)

    with mark("drain"):
        for copy in ag + rs + prod_halo + back_halo + firsts + seconds + thirds:
            copy.wait_send()
        for u in range(UNITS):
            wait_bytes(sbuf.at[u, pl.ds(0, n - 1)], fs.at[u])
            wait_bytes(sbuf2.at[u, pl.ds(0, n - 1)], bs.at[u])
        for copy in leaving:
            copy.wait()


def hand_over(*refs):
    count = (len(refs) - 2) // 3
    srcs, dsts, held = refs[:count], refs[count : 2 * count], refs[2 * count : 3 * count]
    sem_in, sem_out = refs[3 * count :]
    ins, outs = [], []
    for a, b, c in zip(srcs, held, dsts, strict=True):
        pieces = 1
        rows = a.shape[0] // pieces
        for p in range(pieces):
            at, i = pl.ds(p * rows, rows), len(ins)
            ins.append(pltpu.make_async_copy(a.at[at], b.at[at], sem_in.at[i]))
            outs.append(pltpu.make_async_copy(b.at[at], c.at[at], sem_out.at[i]))
    for copy in ins:
        copy.start()
    for arrive, leave in zip(ins, outs, strict=True):
        arrive.wait()
        leave.start()
    for copy in outs:
        copy.wait()


def build(mesh, nx, nz):
    ndp, ny = mesh.shape["dp"], mesh.shape["tensor"]
    n = nx * nz
    finer = Mesh(mesh.devices.reshape(ndp, nx, nz, ny), (DP, CX, CZ, TP))

    def per_device(query, key, value, filters, weight, lengths, plan, out_grad):
        length, width = query.shape[1:]
        groups, taps = filters.shape
        cfg = dict(
            n=n, nx=nx, nz=nz, ny=ny, ndp=ndp, length=length, width=width, taps=taps,
            docs=lengths.shape[1], groups=groups,
        )
        hw, blocks, psz = width // HALVES, length // taps, length // n
        uw = hw // 2
        hbm = pl.BlockSpec(memory_space=pl.ANY)
        dma = pltpu.SemaphoreType.DMA
        row = jax.ShapeDtypeStruct((length, width), BF)
        e = ndp * nx
        assert groups == nz * 8
        outs = pl.pallas_call(
            functools.partial(layer_kernel, cfg),
            name="layer",
            out_shape=[row, row, row, row, jax.ShapeDtypeStruct((nz, 8, taps), F32)],
            in_specs=[hbm] * 8,
            out_specs=[hbm] * 5,
            scratch_shapes=[
                pltpu.SMEM(plan.shape, I32),
                pltpu.SMEM(lengths.shape, I32),
                pltpu.VMEM(plan.shape, I32),
                pltpu.VMEM(filters.shape, BF),
                *[pltpu.VMEM((length, width), BF)] * 4,
                pltpu.VMEM((nz, 8, taps), F32),
                *[pltpu.VMEM((HALVES, 2 * length, uw), BF)] * 2,
                pltpu.VMEM((length, width), BF),
                pltpu.VMEM((length, width), BF),
                pltpu.VMEM(weight.shape, BF),
                pltpu.VMEM((ny, length, width), BF),
                *[pltpu.VMEM((2 * length, 2 * length), BF)] * 4,
                *[pltpu.VMEM((UNITS, n, 2 * psz, uw), BF)] * 4,
                pltpu.VMEM((2 * HALVES, length, uw), BF),
                *[pltpu.VMEM((HALVES, length + taps, hw), BF)] * 2,
                pltpu.VMEM((UNITS, 2 * length, uw), BF),
                pltpu.VMEM((length, width), BF),
                *[pltpu.VMEM((2 * HALVES, length, uw), F32)] * 2,
                pltpu.VMEM((ny, length, width), F32),
                *[pltpu.VMEM((blocks, groups * taps, 2 * taps), BF)] * 2,
                *[pltpu.VMEM((blocks, taps, 2 * taps), F32)] * 3,
                *[pltpu.VMEM((k, length // 2, width), BF) for k in (6, 2, 4)],
                *[pltpu.VMEM((nz, 8, taps), F32)] * 2,
                pltpu.VMEM((e, 8, taps), F32),
                pltpu.VMEM((2, groups, taps), F32),
                dma((4,)), dma((8,)), dma((8,)),
                dma((UNITS,)), dma((UNITS,)),
                dma((6,)), dma((6,)),
                *[dma((HALVES,))] * 4,
                dma((UNITS,)), dma((UNITS,)),
                dma((6,)), dma((6,)),
                dma((nz,)), dma((nz,)),
                dma((e,)), dma((e,)),
                dma((nz,)), dma((nz,)),
            ],
            compiler_params=pltpu.CompilerParams(
                collective_id=0, has_side_effects=True, vmem_limit_bytes=67043328
            ),
        )(plan, lengths, filters, query[0], key[0], value[0], out_grad[0], weight)
        moved = pl.pallas_call(
            hand_over,
            name="results",
            out_shape=[jax.ShapeDtypeStruct(o.shape, o.dtype) for o in outs],
            in_specs=[hbm] * 5,
            out_specs=[hbm] * 5,
            scratch_shapes=[pltpu.VMEM(o.shape, o.dtype) for o in outs] + [dma((17,)), dma((17,))],
        )(*outs)
        mixed, qg, kg, vg, fg = moved
        return mixed[None], qg[None], kg[None], vg[None], fg.reshape(groups, taps)

    rows = P(DP, CONTEXT, TP)
    split = P(TP, None)
    return jax.shard_map(
        per_device,
        mesh=finer,
        in_specs=(rows, rows, rows, split, split, P(DP, None), P(DP, None), rows),
        out_specs=(rows, rows, rows, rows, split),
        check_vma=False,
    )


def solution(mesh):
    return build(mesh, 4, mesh.shape["context"] // 4)
```

```python
import contextlib
import functools
import math

import jax
import jax.numpy as jnp
from jax import lax
from jax.experimental import pallas as pl
from jax.experimental.pallas import tpu as pltpu
from jax.sharding import Mesh
from jax.sharding import PartitionSpec as P

DP, CX, CZ, TP = "dp", "context_0", "context_1", "tensor"
CONTEXT = (CX, CZ)
BF = jnp.bfloat16
F32 = jnp.float32
I32 = jnp.int32
LANES = 128
HALVES = 2
UNITS = 4
MESH_ID = pl.DeviceIdType.MESH
NT = (((1,), (1,)), ((), ()))


def mark(name):
    return contextlib.nullcontext()


def log2(n):
    return n.bit_length() - 1


def iota(shape, dim):
    return lax.broadcasted_iota(I32, shape, dim)


def ones_where(cond):
    return jnp.where(cond, 1.0, 0.0)


def mm(a, b):
    return jnp.dot(a, b, preferred_element_type=F32)


def mm_nt(a, b):
    return lax.dot_general(a, b, NT, preferred_element_type=F32)


def layer_kernel(
    cfg,
    plan_hbm, len_hbm, filt_hbm, q_hbm, k_hbm, v_hbm, og_hbm, w_hbm,
    mixed_h, qg_h, kg_h, vg_h, fg_h,
    plan_s, len_s, plan_v, filt_v, mixed_o, qg_o, kg_o, vg_o, fg_o,
    xp, xq, kv, vv, w, og, fmat, hmat, pmat, rmat, sbuf, rbuf, sbuf2, rbuf2,
    qo, pw, cbw, x2, gated, conv, gg, acc, tf, tb, mf, mb, mflip,
    rs_send, rs_mid, rs_fin, tap, tap1, tap2, tap3,
    small, out_sem, ld, fs, fr, ags, agr, phs, phr, chs, chr_, bs, br, rss, rsr, ts,
):
    n, nx, nz, ny, ndp = cfg["n"], cfg["nx"], cfg["nz"], cfg["ny"], cfg["ndp"]
    length, width, taps, docs = cfg["length"], cfg["width"], cfg["taps"], cfg["docs"]
    psz, gsz, total = length // n, 16, length * n
    hw = width // HALVES
    uw = hw // 2
    cols = hw // LANES
    blocks = length // taps
    per = LANES // gsz
    rows = per * taps
    lgn, lgp = log2(n), log2(psz)

    dp, cx, cz, ty = (lax.axis_index(a) for a in (DP, CX, CZ, TP))
    me = cx * nz + cz
    group_n = ndp * nx
    e_me = dp * nx + cx

    def ctx(index):
        return {CX: index // nz, CZ: lax.rem(index, nz)}

    def peer_e(index):
        return {DP: index // nx, CX: lax.rem(index, nx)}

    def after(k):
        return lax.rem(me + k, n)

    moves = [(k_hbm, kv), (v_hbm, vv), (og_hbm, og.at[ty])]
    for h in range(HALVES):
        for p in range(2):
            moves.append((q_hbm.at[:, pl.ds(h * hw + p * uw, uw)], xq.at[h, pl.ds(p * length, length)]))
    moves.append((w_hbm, w))
    loads = [pltpu.make_async_copy(src, dst, ld.at[i]) for i, (src, dst) in enumerate(moves)]
    small_moves = [(plan_hbm, plan_s), (plan_hbm, plan_v), (filt_hbm, filt_v), (len_hbm, len_s)]
    smalls = [
        pltpu.make_async_copy(src, dst, small.at[i]) for i, (src, dst) in enumerate(small_moves)
    ]
    smalls[0].start()

    barrier = pltpu.get_barrier_semaphore()

    def greet(to):
        pl.semaphore_signal(barrier, inc=1, device_id=to, device_id_type=MESH_ID)

    def far_first(count):
        return sorted(range(count), key=lambda d: -min(d, count - d))

    for dx in far_first(nx):
        for dz in far_first(nz):
            if (dx, dz) != (0, 0):
                greet({CX: lax.rem(cx + dx, nx), CZ: lax.rem(cz + dz, nz)})
    for d in range(1, ndp):
        for k in far_first(nx):
            greet({DP: lax.rem(dp + d, ndp), CX: lax.rem(cx + k, nx)})
    for k in range(1, ny):
        greet({TP: lax.rem(ty + k, ny)})
    greeted = (n - 1) + (ny - 1) + (ndp - 1) * nx
    for load in loads[:2] + smalls[1:] + loads[2:]:
        load.start()

    smalls[0].wait()

    sc = mark('fbuild'); sc.__enter__()
    b = iota((8, 2 * length), 1)
    panel = (b >> lgp) & (n - 1)
    owner = jnp.zeros((8, 2 * length), I32)
    for i in range(n):
        owner = jnp.where(panel == i, plan_s[0, me * n + i] >> lgn, owner)
    target = owner * (2 * psz) + (b >> log2(length)) * psz + (b & (psz - 1))
    square = iota((2 * length, 2 * length), 0)
    fmat[...] = ones_where(square == target[0:1]).astype(BF)
    sc.__exit__(None, None, None)
    with mark('kvwait'):
        for load in loads[:2]:
            load.wait()

    def to_blocks(value):
        return value.astype(BF).reshape(n, 2 * psz, uw)

    for h in range(HALVES):
        for p in range(2):
            at = slice(h * hw + p * uw, h * hw + (p + 1) * uw)
            xp[h, p * length : (p + 1) * length] = (
                kv[:, at].astype(F32) * vv[:, at].astype(F32)
            ).astype(BF)
    def own_blocks(u, x):
        sbuf[u] = to_blocks(mm(fmat[...], x))
        rbuf[u, me] = sbuf[u, me]

    own_blocks(0, xp[0])
    with mark("barrier"):
        pl.semaphore_wait(barrier, greeted)

    def start(src, dst, ssem, rsem, to):
        copy = pltpu.make_async_remote_copy(
            src_ref=src,
            dst_ref=dst,
            send_sem=ssem,
            recv_sem=rsem,
            device_id=to,
            device_id_type=MESH_ID,
        )
        copy.start()
        return copy

    def send_blocks(src, dst, ssem, rsem):
        @pl.loop(0, n - 1)
        def _(k):
            px, pz = lax.rem(k, nx), k // nx
            dx = nx // 2 + ((px + 1) // 2) * (1 - 2 * lax.rem(px, 2))
            dz = nz // 2 + ((pz + 1) // 2) * (1 - 2 * lax.rem(pz, 2))
            x, z = lax.rem(cx + dx, nx), lax.rem(cz + dz, nz)
            start(src.at[x * nz + z], dst.at[me], ssem, rsem, {CX: x, CZ: z})

    def send_forward(u):
        with mark("send"):
            send_blocks(sbuf.at[u], rbuf.at[u], fs, fr.at[u])

    def wait_bytes(ref, sem):
        pltpu.make_async_copy(ref, ref, sem).wait()

    half = length // 2
    up, down = {TP: lax.rem(ty + 1, ny)}, {TP: lax.rem(ty + ny - 1, ny)}
    below, above = lax.rem(ty + ny - 1, ny), lax.rem(ty + 1, ny)
    across = lax.rem(ty + 2, ny)
    first, second = pl.ds(0, half), pl.ds(half, half)

    def pass_on(source, part, to, i):
        piece = og.at[source, part]
        return start(piece, piece, ags.at[i], agr.at[i], to)

    send_forward(0)
    loads[2].wait()
    ag = [
        pass_on(ty, first, up, 0),
        pass_on(ty, second, down, 1),
        pass_on(ty, second, up, 2),
        pass_on(ty, first, down, 3),
    ]
    own_blocks(1, xp[1])
    send_forward(1)
    for h in range(HALVES):
        for load in loads[3 + 2 * h : 5 + 2 * h]:
            load.wait()
        own_blocks(HALVES + h, xq[h])

    for load in smalls[1:]:
        load.wait()
    pv = plan_v[...]
    slot_of = jnp.where((pv >> lgn) == me, pv & (n - 1), 0).astype(F32)
    slot_of = jnp.broadcast_to(slot_of, (8, n * n)).astype(BF)
    table = (n * n, 2 * length)
    gather = ones_where((iota(table, 0) >> lgn) == (iota(table, 1) >> (lgp + 1)))
    slot = mm(slot_of, gather.astype(BF)).astype(I32)
    target = ((b >> lgp) & 1) * length + slot * psz + (b & (psz - 1))
    pmat[...] = ones_where(square == target[0:1]).astype(BF)

    starts = []
    run = jnp.int32(0)
    for d in range(docs):
        starts.append(run)
        run = run + len_s[0, d]

    def documents(positions):
        count = jnp.zeros(positions.shape, I32)
        for begin in starts:
            count = count + jnp.where(positions >= begin, 1, 0)
        return jnp.where(positions >= total, docs + 1, count)

    base = me * length
    row = iota((taps, LANES), 0)
    lane = iota((taps, LANES), 1)
    lane8 = iota((8, (blocks + 2) * taps), 1)
    along = documents(base - taps + lane8)

    def same(doc_rows, at):
        return doc_rows == along[0:1, at : at + taps]

    for k in range(blocks):
        here = documents(base + k * taps + row)
        at = (k + 1) * taps
        mf[k, :, 0:taps] = ones_where(same(here, at - taps) & (lane > row))
        mf[k, :, taps : 2 * taps] = ones_where(same(here, at) & (lane <= row))
        mb[k, :, 0:taps] = ones_where(same(here, at) & (lane >= row))
        mb[k, :, taps : 2 * taps] = ones_where(same(here, at + taps) & (lane < row))
        back = taps - 1 - row
        here = documents(base + k * taps + back)
        mflip[k, :, 0:taps] = ones_where(same(here, at - taps) & (lane > back))
        mflip[k, :, taps : 2 * taps] = ones_where(same(here, at) & (lane <= back))

    filt = filt_v[...]
    turn = ones_where(((taps - row) & (taps - 1)) == lane).astype(BF)
    tap3[0] = filt.astype(F32)
    tap3[1] = mm(filt, turn)

    def circulants(t_ref, m_ref, which):
        with mark("toep"):

            @pl.loop(0, cfg["groups"], step=4)
            def _(first_group):
                for i in range(4):
                    g = first_group + i
                    taps_row = jnp.broadcast_to(tap3[which, pl.ds(g, 1), :], (taps, taps))
                    circ = pltpu.roll(taps_row, 0, 1, stride=1, stride_axis=0)
                    at = pl.ds(pl.multiple_of(g * taps, taps), taps)
                    for k in range(blocks):
                        for h in range(2):
                            part = slice(h * taps, (h + 1) * taps)
                            t_ref[k, at, part] = (circ * m_ref[k, :, part]).astype(BF)

    def add_grad(source, opening):
        with mark("gg"):

            @pl.loop(0, 2 * HALVES)
            def _(c):
                part = mm_nt(
                    og[source],
                    w[
                        pl.ds(pl.multiple_of(c * uw, uw), uw),
                        pl.ds(pl.multiple_of(source * width, width), width),
                    ],
                )
                gg[c] = part if opening else gg[c] + part

    nxt, prv = ctx(after(1)), ctx(after(n - 1))
    prod_halo, back_halo = [], []

    def arrived(u):
        with mark(f"fwait{u}"):
            wait_bytes(rbuf.at[u, pl.ds(0, n - 1)], fr.at[u])
        owned = mm(pmat[...], rbuf[u].reshape(2 * length, uw)).astype(BF)
        return owned[0:length], owned[length : 2 * length]

    def receive_product(h):
        pw[h, taps : taps + length, 0:uw], pw[h, taps : taps + length, uw:hw] = arrived(h)
        prod_halo.append(
            start(pw.at[h, pl.ds(length, taps)], pw.at[h, pl.ds(0, taps)], phs.at[h], phr.at[h], nxt)
        )
        send_forward(HALVES + h)

    def receive_query(h):
        for p, part in enumerate(arrived(HALVES + h)):
            qo[2 * h + p] = part
            cbw[h, 0:length, p * uw : (p + 1) * uw] = (
                gg[2 * h + p] * part.astype(F32)
            ).astype(BF)
        back_halo.append(
            start(cbw.at[h, pl.ds(0, taps)], cbw.at[h, pl.ds(length, taps)], chs.at[h], chr_.at[h], prv)
        )

    group = lane >> log2(gsz)
    anti = ones_where(lane == taps - 1 - row).astype(BF)

    def pick(res):
        out = res[0:taps]
        for g in range(1, per):
            out = jnp.where(group == g, res[g * taps : (g + 1) * taps], out)
        return out

    def each_tile(h):
        for j in range(cols):
            lanes = slice(j * LANES, (j + 1) * LANES)
            col = h * cols + j
            for k in range(blocks):
                own = slice(k * taps, (k + 1) * taps)
                win = slice(k * taps, (k + 2) * taps)
                yield j, col, k, lanes, own, win, slice(col * rows, (col + 1) * rows)

    def placed(j, k):
        p, at = (j * LANES) // uw, (j * LANES) % uw
        return p, slice(p * length + k * taps, p * length + (k + 1) * taps), slice(at, at + LANES)

    def filter_forward(h):
        with mark(f"phalo{h}"):
            prod_halo[h].wait_recv()
        with mark("conv"):
            for j, col, k, lanes, own, win, t_rows in each_tile(h):
                p, _, at = placed(j, k)
                conv[2 * h + p, own, at] = pick(mm(tf[k, t_rows, :], pw[h, win, lanes]))

    def pack_back(u):
        sbuf2[u] = to_blocks(mm(rmat[...], x2[u]))
        rbuf2[u, me] = sbuf2[u, me]

    def query_back(h):
        with mark("qback"):
            for p in range(2):
                x2[h, p * length : (p + 1) * length] = (gg[2 * h + p] * conv[2 * h + p]).astype(BF)
            pack_back(h)

    def gate(h):
        for p in range(2):
            at = slice(h * hw + p * uw, h * hw + (p + 1) * uw)
            gated[:, at] = (qo[2 * h + p].astype(F32) * conv[2 * h + p]).astype(BF)

    def project(y, h):
        at = pl.ds(pl.multiple_of(y * width, width), width)
        rows_in = slice(h * hw, (h + 1) * hw)
        return mm(gated[:, rows_in], w[rows_in, at])

    def product_back(h):
        u = HALVES + h
        with mark(f"chalo{h}"):
            back_halo[h].wait_recv()
        with mark("pback"):
            for j, _, k, lanes, _, win, t_rows in each_tile(h):
                _, to, at = placed(j, k)
                x2[u, to, at] = pick(mm(tb[k, t_rows, :], cbw[h, win, lanes])).astype(BF)
            pack_back(u)

    def send_back(u):
        with mark("send2"):
            send_blocks(sbuf2.at[u], rbuf2.at[u], bs, br.at[u])

    def filter_terms(h):
        with mark("terms"):
            for _, col, k, lanes, own, win, _ in each_tile(h):
                if k == 0:
                    outer = [None] * per
                flipped = mm(anti, cbw[h, own, lanes])
                stacked = jnp.concatenate(
                    [jnp.where(group == g, flipped, 0.0).astype(BF) for g in range(per)], axis=0
                )
                res = mm_nt(stacked, pw[h, win, lanes])
                for g in range(per):
                    part = res[g * taps : (g + 1) * taps]
                    term = (
                        part[:, 0:taps] * mflip[k, :, 0:taps]
                        + part[:, taps:] * mflip[k, :, taps:]
                    )
                    outer[g] = term if k == 0 else outer[g] + term
                if k == blocks - 1:
                    turned = [pltpu.roll(o, 0, 1, stride=1, stride_axis=0) for o in outer]
                    tap[col] = jnp.concatenate(
                        [jnp.sum(o, axis=0, keepdims=True) for o in turned], axis=0
                    )

    circulants(tf, mf, 1)
    with mark("wwait"):
        loads[-1].wait()
    add_grad(ty, True)
    receive_product(0)
    with mark("agw"):
        ag[0].wait_recv()
        ag.append(pass_on(below, first, up, 4))
        ag[1].wait_recv()
        ag.append(pass_on(above, second, down, 5))
    eye = ones_where(square == iota((2 * length, 2 * length), 1)).astype(BF)
    rmat[...] = mm_nt(eye, pmat[...]).astype(BF)
    hmat[...] = mm_nt(eye, fmat[...]).astype(BF)
    circulants(tb, mb, 0)
    receive_product(1)
    with mark("agw2"):
        ag[2].wait_recv()
        ag[3].wait_recv()
    add_grad(below, False)
    add_grad(above, False)
    filter_forward(0)
    with mark("agw3"):
        ag[4].wait_recv()
        ag[5].wait_recv()
    add_grad(across, False)
    query_back(0)
    send_back(0)
    receive_query(0)
    gate(0)
    with mark("proj"):

        @pl.loop(0, ny)
        def _(y):
            acc[y] = project(y, 0)

    filter_terms(0)
    filter_forward(1)
    query_back(1)
    receive_query(1)
    gate(1)

    filter_terms(1)
    for k in range(1, nz):
        to = lax.rem(cz + k, nz)
        start(tap.at[to], tap1.at[cz], ts.at[0], ts.at[1], {CZ: to})
    tap1[cz] = tap[cz]
    send_back(1)

    lo, hi = slice(0, half), slice(half, length)

    def reduce_send(i, dst, to):
        return start(rs_send.at[i], dst, rss.at[i], rsr.at[i], to)

    with mark("proj"):
        part = acc[across] + project(across, 1)
        rs_send[0] = part[lo].astype(BF)
        rs_send[1] = part[hi].astype(BF)
        rs = [reduce_send(0, rs_mid.at[0], up), reduce_send(1, rs_mid.at[1], down)]
        part = acc[above] + project(above, 1)
        rs_send[2] = part[hi].astype(BF)
        rs.append(reduce_send(2, rs_fin.at[0], up))
        acc[above, lo] = part[lo]
        part = acc[below] + project(below, 1)
        rs_send[3] = part[lo].astype(BF)
        rs.append(reduce_send(3, rs_fin.at[1], down))
        acc[below, hi] = part[hi]
        acc[ty] = (acc[ty] + project(ty, 1)).astype(BF).astype(F32)

    product_back(0)
    send_back(2)
    product_back(1)
    with mark("t1wait"):
        wait_bytes(tap1.at[pl.ds(0, nz - 1)], ts.at[1])
    tap2[e_me] = jnp.sum(tap1[...], axis=0)
    for k in range(1, group_n):
        to = peer_e(lax.rem(e_me + k, group_n))
        start(tap2.at[e_me], tap2.at[e_me], ts.at[2], ts.at[3], to)
    send_back(3)
    with mark("rsmid"):
        rs[0].wait_recv()
        rs_send[4] = (acc[above, lo] + rs_mid[0].astype(F32)).astype(BF)
        rs.append(reduce_send(4, rs_fin.at[2], up))
        rs[1].wait_recv()
        rs_send[5] = (acc[below, hi] + rs_mid[1].astype(F32)).astype(BF)
        rs.append(reduce_send(5, rs_fin.at[3], down))

    leaving = []

    def leave(src, dst):
        copy = pltpu.make_async_copy(src, dst, out_sem.at[len(leaving)])
        copy.start()
        leaving.append(copy)

    def loader_rows(u):
        h = u % HALVES
        with mark(f"bwait{u}"):
            wait_bytes(rbuf2.at[u, pl.ds(0, n - 1)], br.at[u])
        home = mm(hmat[...], rbuf2[u].reshape(2 * length, uw))
        for p in range(2):
            part = home[p * length : (p + 1) * length]
            at = slice(h * hw + p * uw, h * hw + (p + 1) * uw)
            if u < HALVES:
                qg_o[:, at] = part.astype(BF)
            else:
                kg_o[:, at] = (part * vv[:, at].astype(F32)).astype(BF)
                vg_o[:, at] = (part * kv[:, at].astype(F32)).astype(BF)
        at = pl.ds(h * hw, hw)
        for held, out in [(qg_o, qg_h)] if u < HALVES else [(kg_o, kg_h), (vg_o, vg_h)]:
            leave(held.at[:, at], out.at[:, at])

    loader_rows(0)
    with mark("t2wait"):
        wait_bytes(tap2.at[pl.ds(0, group_n - 1)], ts.at[3])
    summed = tap2[0]
    for i in range(1, group_n):
        summed = summed + tap2[i]
    scale = 1.0 / math.sqrt(float(ndp * total))
    mirror = ones_where(lane == taps - 1 - row)
    fg_o[cz] = scale * jnp.dot(
        summed, mirror, precision=lax.Precision.HIGHEST, preferred_element_type=F32
    )
    for k in range(1, nz):
        to = {CZ: lax.rem(cz + k, nz)}
        start(fg_o.at[cz], fg_o.at[cz], ts.at[4], ts.at[5], to)
    loader_rows(1)
    loader_rows(2)
    with mark("rswait"):
        for copy in rs[2:]:
            copy.wait_recv()
    for rows_of, one, two in ((lo, 1, 2), (hi, 0, 3)):
        summed = acc[ty, rows_of] + rs_fin[one].astype(F32) + rs_fin[two].astype(F32)
        mixed_o[rows_of] = summed.astype(BF)
    leave(mixed_o, mixed_h)
    loader_rows(3)
    with mark("t3wait"):
        wait_bytes(fg_o.at[pl.ds(0, nz - 1)], ts.at[5])
    leave(fg_o, fg_h)

    with mark("drain"):
        for copy in ag + rs + prod_halo + back_halo:
            copy.wait_send()
        wait_bytes(tap1.at[pl.ds(0, nz - 1)], ts.at[0])
        wait_bytes(tap2.at[pl.ds(0, group_n - 1)], ts.at[2])
        wait_bytes(fg_o.at[pl.ds(0, nz - 1)], ts.at[4])
        wait_bytes(sbuf.at[:, pl.ds(0, n - 1)], fs)
        wait_bytes(sbuf2.at[:, pl.ds(0, n - 1)], bs)
        for copy in leaving:
            copy.wait()


def hand_over(*refs):
    count = (len(refs) - 2) // 3
    srcs, dsts, held = refs[:count], refs[count : 2 * count], refs[2 * count : 3 * count]
    sem_in, sem_out = refs[3 * count :]
    ins, outs = [], []
    for a, b, c in zip(srcs, held, dsts, strict=True):
        pieces = 1
        rows = a.shape[0] // pieces
        for p in range(pieces):
            at, i = pl.ds(p * rows, rows), len(ins)
            ins.append(pltpu.make_async_copy(a.at[at], b.at[at], sem_in.at[i]))
            outs.append(pltpu.make_async_copy(b.at[at], c.at[at], sem_out.at[i]))
    for copy in ins:
        copy.start()
    for arrive, leave in zip(ins, outs, strict=True):
        arrive.wait()
        leave.start()
    for copy in outs:
        copy.wait()


def build(mesh, nx, nz):
    ndp, ny = mesh.shape["dp"], mesh.shape["tensor"]
    n = nx * nz
    finer = Mesh(mesh.devices.reshape(ndp, nx, nz, ny), (DP, CX, CZ, TP))

    def per_device(query, key, value, filters, weight, lengths, plan, out_grad):
        length, width = query.shape[1:]
        groups, taps = filters.shape
        cfg = dict(
            n=n, nx=nx, nz=nz, ny=ny, ndp=ndp, length=length, width=width, taps=taps,
            docs=lengths.shape[1], groups=groups,
        )
        hw, blocks, psz = width // HALVES, length // taps, length // n
        uw = hw // 2
        hbm = pl.BlockSpec(memory_space=pl.ANY)
        dma = pltpu.SemaphoreType.DMA
        row = jax.ShapeDtypeStruct((length, width), BF)
        e = ndp * nx
        assert groups == nz * 8
        outs = pl.pallas_call(
            functools.partial(layer_kernel, cfg),
            name="layer",
            out_shape=[row, row, row, row, jax.ShapeDtypeStruct((nz, 8, taps), F32)],
            in_specs=[hbm] * 8,
            out_specs=[hbm] * 5,
            scratch_shapes=[
                pltpu.SMEM(plan.shape, I32),
                pltpu.SMEM(lengths.shape, I32),
                pltpu.VMEM(plan.shape, I32),
                pltpu.VMEM(filters.shape, BF),
                *[pltpu.VMEM((length, width), BF)] * 4,
                pltpu.VMEM((nz, 8, taps), F32),
                *[pltpu.VMEM((HALVES, 2 * length, uw), BF)] * 2,
                pltpu.VMEM((length, width), BF),
                pltpu.VMEM((length, width), BF),
                pltpu.VMEM(weight.shape, BF),
                pltpu.VMEM((ny, length, width), BF),
                *[pltpu.VMEM((2 * length, 2 * length), BF)] * 4,
                *[pltpu.VMEM((UNITS, n, 2 * psz, uw), BF)] * 4,
                pltpu.VMEM((2 * HALVES, length, uw), BF),
                *[pltpu.VMEM((HALVES, length + taps, hw), BF)] * 2,
                pltpu.VMEM((UNITS, 2 * length, uw), BF),
                pltpu.VMEM((length, width), BF),
                *[pltpu.VMEM((2 * HALVES, length, uw), F32)] * 2,
                pltpu.VMEM((ny, length, width), F32),
                *[pltpu.VMEM((blocks, groups * taps, 2 * taps), BF)] * 2,
                *[pltpu.VMEM((blocks, taps, 2 * taps), F32)] * 3,
                *[pltpu.VMEM((k, length // 2, width), BF) for k in (6, 2, 4)],
                *[pltpu.VMEM((nz, 8, taps), F32)] * 2,
                pltpu.VMEM((e, 8, taps), F32),
                pltpu.VMEM((2, groups, taps), F32),
                dma((4,)), dma((8,)), dma((8,)),
                dma, dma((UNITS,)),
                dma((6,)), dma((6,)),
                *[dma((HALVES,))] * 4,
                dma, dma((UNITS,)),
                dma((6,)), dma((6,)),
                dma((6,)),
            ],
            compiler_params=pltpu.CompilerParams(
                collective_id=0, has_side_effects=True, vmem_limit_bytes=67043328
            ),
        )(plan, lengths, filters, query[0], key[0], value[0], out_grad[0], weight)
        moved = pl.pallas_call(
            hand_over,
            name="results",
            out_shape=[jax.ShapeDtypeStruct(o.shape, o.dtype) for o in outs],
            in_specs=[hbm] * 5,
            out_specs=[hbm] * 5,
            scratch_shapes=[pltpu.VMEM(o.shape, o.dtype) for o in outs] + [dma((5,)), dma((5,))],
        )(*outs)
        mixed, qg, kg, vg, fg = moved
        return mixed[None], qg[None], kg[None], vg[None], fg.reshape(groups, taps)

    rows = P(DP, CONTEXT, TP)
    split = P(TP, None)
    return jax.shard_map(
        per_device,
        mesh=finer,
        in_specs=(rows, rows, rows, split, split, P(DP, None), P(DP, None), rows),
        out_specs=(rows, rows, rows, rows, split),
        check_vma=False,
    )


def solution(mesh):
    return build(mesh, 4, mesh.shape["context"] // 4)
```

```python
import contextlib
import functools
import math

import jax
import jax.numpy as jnp
from jax import lax
from jax.experimental import pallas as pl
from jax.experimental.pallas import tpu as pltpu
from jax.sharding import Mesh
from jax.sharding import PartitionSpec as P

DP, CX, CZ, TP = "dp", "context_0", "context_1", "tensor"
CONTEXT = (CX, CZ)
BF = jnp.bfloat16
F32 = jnp.float32
I32 = jnp.int32
LANES = 128
HALVES = 2
UNITS = 4
MESH_ID = pl.DeviceIdType.MESH
NT = (((1,), (1,)), ((), ()))


def mark(name):
    return contextlib.nullcontext()


def log2(n):
    return n.bit_length() - 1


def iota(shape, dim):
    return lax.broadcasted_iota(I32, shape, dim)


def ones_where(cond):
    return jnp.where(cond, 1.0, 0.0)


def mm(a, b):
    return jnp.dot(a, b, preferred_element_type=F32)


def mm_nt(a, b):
    return lax.dot_general(a, b, NT, preferred_element_type=F32)


def layer_kernel(
    cfg,
    plan_hbm, len_hbm, filt_hbm, q_hbm, k_hbm, v_hbm, og_hbm, w_hbm,
    mixed_h, qg_h, kg_h, vg_h, fg_h,
    plan_s, len_s, plan_v, filt_v, mixed_o, qg_o, kg_o, vg_o, fg_o,
    xp, xq, kv, vv, w, og, fmat, hmat, pmat, rmat, sbuf, rbuf, sbuf2, rbuf2,
    qo, pw, cbw, x2, gated, conv, gg, acc, tf, tb, mf, mb, mflip,
    rs_send, rs_mid, rs_fin, tap, tap1, tap2, tap3,
    small, out_sem, ld, fs, fr, ags, agr, phs, phr, chs, chr_, bs, br, rss, rsr, ts,
):
    n, nx, nz, ny, ndp = cfg["n"], cfg["nx"], cfg["nz"], cfg["ny"], cfg["ndp"]
    length, width, taps, docs = cfg["length"], cfg["width"], cfg["taps"], cfg["docs"]
    psz, gsz, total = length // n, 16, length * n
    hw = width // HALVES
    uw = hw // 2
    cols = hw // LANES
    blocks = length // taps
    per = LANES // gsz
    rows = per * taps
    lgn, lgp = log2(n), log2(psz)

    dp, cx, cz, ty = (lax.axis_index(a) for a in (DP, CX, CZ, TP))
    me = cx * nz + cz
    group_n = ndp * nx
    e_me = dp * nx + cx

    def ctx(index):
        return {CX: index // nz, CZ: lax.rem(index, nz)}

    def peer_e(index):
        return {DP: index // nx, CX: lax.rem(index, nx)}

    def after(k):
        return lax.rem(me + k, n)

    moves = [(k_hbm, kv), (v_hbm, vv), (og_hbm, og.at[ty])]
    for h in range(HALVES):
        for p in range(2):
            moves.append((q_hbm.at[:, pl.ds(h * hw + p * uw, uw)], xq.at[h, pl.ds(p * length, length)]))
    moves.append((w_hbm, w))
    loads = [pltpu.make_async_copy(src, dst, ld.at[i]) for i, (src, dst) in enumerate(moves)]
    small_moves = [(plan_hbm, plan_s), (plan_hbm, plan_v), (filt_hbm, filt_v), (len_hbm, len_s)]
    smalls = [
        pltpu.make_async_copy(src, dst, small.at[i]) for i, (src, dst) in enumerate(small_moves)
    ]
    smalls[0].start()

    barrier = pltpu.get_barrier_semaphore()

    def greet(to):
        pl.semaphore_signal(barrier, inc=1, device_id=to, device_id_type=MESH_ID)

    def far_first(count):
        return sorted(range(count), key=lambda d: -min(d, count - d))

    for dx in far_first(nx):
        for dz in far_first(nz):
            if (dx, dz) != (0, 0):
                greet({CX: lax.rem(cx + dx, nx), CZ: lax.rem(cz + dz, nz)})
    for d in range(1, ndp):
        for k in far_first(nx):
            greet({DP: lax.rem(dp + d, ndp), CX: lax.rem(cx + k, nx)})
    for k in range(1, ny):
        greet({TP: lax.rem(ty + k, ny)})
    greeted = (n - 1) + (ny - 1) + (ndp - 1) * nx
    for load in loads[:2] + smalls[1:] + loads[2:]:
        load.start()

    smalls[0].wait()

    sc = mark('fbuild'); sc.__enter__()
    b = iota((8, 2 * length), 1)
    panel = (b >> lgp) & (n - 1)
    owner = jnp.zeros((8, 2 * length), I32)
    for i in range(n):
        owner = jnp.where(panel == i, plan_s[0, me * n + i] >> lgn, owner)
    target = owner * (2 * psz) + (b >> log2(length)) * psz + (b & (psz - 1))
    square = iota((2 * length, 2 * length), 0)
    fmat[...] = ones_where(square == target[0:1]).astype(BF)
    sc.__exit__(None, None, None)
    with mark('kvwait'):
        for load in loads[:2]:
            load.wait()

    def to_blocks(value):
        return value.astype(BF).reshape(n, 2 * psz, uw)

    for h in range(HALVES):
        for p in range(2):
            at = slice(h * hw + p * uw, h * hw + (p + 1) * uw)
            xp[h, p * length : (p + 1) * length] = (
                kv[:, at].astype(F32) * vv[:, at].astype(F32)
            ).astype(BF)
    def own_blocks(u, x):
        sbuf[u] = to_blocks(mm(fmat[...], x))
        rbuf[u, me] = sbuf[u, me]

    own_blocks(0, xp[0])
    with mark("barrier"):
        pl.semaphore_wait(barrier, greeted)

    def start(src, dst, ssem, rsem, to):
        copy = pltpu.make_async_remote_copy(
            src_ref=src,
            dst_ref=dst,
            send_sem=ssem,
            recv_sem=rsem,
            device_id=to,
            device_id_type=MESH_ID,
        )
        copy.start()
        return copy

    def send_blocks(src, dst, ssem, rsem):
        @pl.loop(0, n - 1)
        def _(k):
            px, pz = lax.rem(k, nx), k // nx
            dx = nx // 2 + ((px + 1) // 2) * (1 - 2 * lax.rem(px, 2))
            dz = nz // 2 + ((pz + 1) // 2) * (1 - 2 * lax.rem(pz, 2))
            x, z = lax.rem(cx + dx, nx), lax.rem(cz + dz, nz)
            start(src.at[x * nz + z], dst.at[me], ssem, rsem, {CX: x, CZ: z})

    def send_forward(u):
        with mark("send"):
            send_blocks(sbuf.at[u], rbuf.at[u], fs, fr.at[u])

    def wait_bytes(ref, sem):
        pltpu.make_async_copy(ref, ref, sem).wait()

    half = length // 2
    up, down = {TP: lax.rem(ty + 1, ny)}, {TP: lax.rem(ty + ny - 1, ny)}
    below, above = lax.rem(ty + ny - 1, ny), lax.rem(ty + 1, ny)
    across = lax.rem(ty + 2, ny)
    first, second = pl.ds(0, half), pl.ds(half, half)

    def pass_on(source, part, to, i):
        piece = og.at[source, part]
        return start(piece, piece, ags.at[i], agr.at[i], to)

    send_forward(0)
    loads[2].wait()
    ag = [
        pass_on(ty, first, up, 0),
        pass_on(ty, second, down, 1),
        pass_on(ty, second, up, 2),
        pass_on(ty, first, down, 3),
    ]
    own_blocks(1, xp[1])
    send_forward(1)
    for h in range(HALVES):
        for load in loads[3 + 2 * h : 5 + 2 * h]:
            load.wait()
        own_blocks(HALVES + h, xq[h])

    for load in smalls[1:]:
        load.wait()
    pv = plan_v[...]
    slot_of = jnp.where((pv >> lgn) == me, pv & (n - 1), 0).astype(F32)
    slot_of = jnp.broadcast_to(slot_of, (8, n * n)).astype(BF)
    table = (n * n, 2 * length)
    gather = ones_where((iota(table, 0) >> lgn) == (iota(table, 1) >> (lgp + 1)))
    slot = mm(slot_of, gather.astype(BF)).astype(I32)
    target = ((b >> lgp) & 1) * length + slot * psz + (b & (psz - 1))
    pmat[...] = ones_where(square == target[0:1]).astype(BF)

    starts = []
    run = jnp.int32(0)
    for d in range(docs):
        starts.append(run)
        run = run + len_s[0, d]

    def documents(positions):
        count = jnp.zeros(positions.shape, I32)
        for begin in starts:
            count = count + jnp.where(positions >= begin, 1, 0)
        return jnp.where(positions >= total, docs + 1, count)

    base = me * length
    row = iota((taps, LANES), 0)
    lane = iota((taps, LANES), 1)
    lane8 = iota((8, (blocks + 2) * taps), 1)
    along = documents(base - taps + lane8)

    def same(doc_rows, at):
        return doc_rows == along[0:1, at : at + taps]

    for k in range(blocks):
        here = documents(base + k * taps + row)
        at = (k + 1) * taps
        mf[k, :, 0:taps] = ones_where(same(here, at - taps) & (lane > row))
        mf[k, :, taps : 2 * taps] = ones_where(same(here, at) & (lane <= row))
        mb[k, :, 0:taps] = ones_where(same(here, at) & (lane >= row))
        mb[k, :, taps : 2 * taps] = ones_where(same(here, at + taps) & (lane < row))
        back = taps - 1 - row
        here = documents(base + k * taps + back)
        mflip[k, :, 0:taps] = ones_where(same(here, at - taps) & (lane > back))
        mflip[k, :, taps : 2 * taps] = ones_where(same(here, at) & (lane <= back))

    filt = filt_v[...]
    turn = ones_where(((taps - row) & (taps - 1)) == lane).astype(BF)
    tap3[0] = filt.astype(F32)
    tap3[1] = mm(filt, turn)

    def circulants(t_ref, m_ref, which):
        with mark("toep"):

            @pl.loop(0, cfg["groups"], step=4)
            def _(first_group):
                for i in range(4):
                    g = first_group + i
                    taps_row = jnp.broadcast_to(tap3[which, pl.ds(g, 1), :], (taps, taps))
                    circ = pltpu.roll(taps_row, 0, 1, stride=1, stride_axis=0)
                    at = pl.ds(pl.multiple_of(g * taps, taps), taps)
                    for k in range(blocks):
                        for h in range(2):
                            part = slice(h * taps, (h + 1) * taps)
                            t_ref[k, at, part] = (circ * m_ref[k, :, part]).astype(BF)

    def add_grad(source, opening):
        with mark("gg"):

            @pl.loop(0, 2 * HALVES)
            def _(c):
                part = mm_nt(
                    og[source],
                    w[
                        pl.ds(pl.multiple_of(c * uw, uw), uw),
                        pl.ds(pl.multiple_of(source * width, width), width),
                    ],
                )
                gg[c] = part if opening else gg[c] + part

    nxt, prv = ctx(after(1)), ctx(after(n - 1))
    prod_halo, back_halo = [], []

    def arrived(u):
        with mark(f"fwait{u}"):
            wait_bytes(rbuf.at[u, pl.ds(0, n - 1)], fr.at[u])
        owned = mm(pmat[...], rbuf[u].reshape(2 * length, uw)).astype(BF)
        return owned[0:length], owned[length : 2 * length]

    def receive_product(h):
        pw[h, taps : taps + length, 0:uw], pw[h, taps : taps + length, uw:hw] = arrived(h)
        prod_halo.append(
            start(pw.at[h, pl.ds(length, taps)], pw.at[h, pl.ds(0, taps)], phs.at[h], phr.at[h], nxt)
        )
        send_forward(HALVES + h)

    def receive_query(h):
        for p, part in enumerate(arrived(HALVES + h)):
            qo[2 * h + p] = part
            cbw[h, 0:length, p * uw : (p + 1) * uw] = (
                gg[2 * h + p] * part.astype(F32)
            ).astype(BF)
        back_halo.append(
            start(cbw.at[h, pl.ds(0, taps)], cbw.at[h, pl.ds(length, taps)], chs.at[h], chr_.at[h], prv)
        )

    group = lane >> log2(gsz)
    anti = ones_where(lane == taps - 1 - row).astype(BF)

    def pick(res):
        out = res[0:taps]
        for g in range(1, per):
            out = jnp.where(group == g, res[g * taps : (g + 1) * taps], out)
        return out

    def each_tile(h):
        for j in range(cols):
            lanes = slice(j * LANES, (j + 1) * LANES)
            col = h * cols + j
            for k in range(blocks):
                own = slice(k * taps, (k + 1) * taps)
                win = slice(k * taps, (k + 2) * taps)
                yield j, col, k, lanes, own, win, slice(col * rows, (col + 1) * rows)

    def placed(j, k):
        p, at = (j * LANES) // uw, (j * LANES) % uw
        return p, slice(p * length + k * taps, p * length + (k + 1) * taps), slice(at, at + LANES)

    def filter_forward(h):
        with mark(f"phalo{h}"):
            prod_halo[h].wait_recv()
        with mark("conv"):
            for j, col, k, lanes, own, win, t_rows in each_tile(h):
                p, _, at = placed(j, k)
                conv[2 * h + p, own, at] = pick(mm(tf[k, t_rows, :], pw[h, win, lanes]))

    def pack_back(u):
        sbuf2[u] = to_blocks(mm(rmat[...], x2[u]))
        rbuf2[u, me] = sbuf2[u, me]

    def query_back(h):
        with mark("qback"):
            for p in range(2):
                x2[h, p * length : (p + 1) * length] = (gg[2 * h + p] * conv[2 * h + p]).astype(BF)
            pack_back(h)

    def gate(h):
        for p in range(2):
            at = slice(h * hw + p * uw, h * hw + (p + 1) * uw)
            gated[:, at] = (qo[2 * h + p].astype(F32) * conv[2 * h + p]).astype(BF)

    def project(y, h):
        at = pl.ds(pl.multiple_of(y * width, width), width)
        rows_in = slice(h * hw, (h + 1) * hw)
        return mm(gated[:, rows_in], w[rows_in, at])

    def product_back(h):
        u = HALVES + h
        with mark(f"chalo{h}"):
            back_halo[h].wait_recv()
        with mark("pback"):
            for j, _, k, lanes, _, win, t_rows in each_tile(h):
                _, to, at = placed(j, k)
                x2[u, to, at] = pick(mm(tb[k, t_rows, :], cbw[h, win, lanes])).astype(BF)
            pack_back(u)

    def send_back(u):
        with mark("send2"):
            send_blocks(sbuf2.at[u], rbuf2.at[u], bs, br.at[u])

    def filter_terms(h):
        with mark("terms"):
            for _, col, k, lanes, own, win, _ in each_tile(h):
                if k == 0:
                    outer = [None] * per
                flipped = mm(anti, cbw[h, own, lanes])
                stacked = jnp.concatenate(
                    [jnp.where(group == g, flipped, 0.0).astype(BF) for g in range(per)], axis=0
                )
                res = mm_nt(stacked, pw[h, win, lanes])
                for g in range(per):
                    part = res[g * taps : (g + 1) * taps]
                    term = (
                        part[:, 0:taps] * mflip[k, :, 0:taps]
                        + part[:, taps:] * mflip[k, :, taps:]
                    )
                    outer[g] = term if k == 0 else outer[g] + term
                if k == blocks - 1:
                    turned = [pltpu.roll(o, 0, 1, stride=1, stride_axis=0) for o in outer]
                    tap[col] = jnp.concatenate(
                        [jnp.sum(o, axis=0, keepdims=True) for o in turned], axis=0
                    )

    circulants(tf, mf, 1)
    with mark("wwait"):
        loads[-1].wait()
    add_grad(ty, True)
    receive_product(0)
    with mark("agw"):
        ag[0].wait_recv()
        ag.append(pass_on(below, first, up, 4))
        ag[1].wait_recv()
        ag.append(pass_on(above, second, down, 5))
    eye = ones_where(square == iota((2 * length, 2 * length), 1)).astype(BF)
    rmat[...] = mm_nt(eye, pmat[...]).astype(BF)
    hmat[...] = mm_nt(eye, fmat[...]).astype(BF)
    circulants(tb, mb, 0)
    receive_product(1)
    with mark("agw2"):
        ag[2].wait_recv()
        ag[3].wait_recv()
    add_grad(below, False)
    add_grad(above, False)
    filter_forward(0)
    with mark("agw3"):
        ag[4].wait_recv()
        ag[5].wait_recv()
    add_grad(across, False)
    query_back(0)
    send_back(0)
    receive_query(0)
    gate(0)
    with mark("proj"):

        @pl.loop(0, ny)
        def _(y):
            acc[y] = project(y, 0)

    filter_terms(0)
    filter_forward(1)
    query_back(1)
    receive_query(1)
    gate(1)

    lo, hi = slice(0, half), slice(half, length)

    def reduce_send(i, dst, to):
        return start(rs_send.at[i], dst, rss.at[i], rsr.at[i], to)

    with mark("across"):
        part = acc[across] + project(across, 1)
        rs_send[0] = part[lo].astype(BF)
        rs_send[1] = part[hi].astype(BF)
        rs = [reduce_send(0, rs_mid.at[0], up), reduce_send(1, rs_mid.at[1], down)]

    filter_terms(1)
    for k in range(1, nz):
        to = lax.rem(cz + k, nz)
        start(tap.at[to], tap1.at[cz], ts.at[0], ts.at[1], {CZ: to})
    tap1[cz] = tap[cz]
    send_back(1)

    with mark("proj"):
        part = acc[above] + project(above, 1)
        rs_send[2] = part[hi].astype(BF)
        rs.append(reduce_send(2, rs_fin.at[0], up))
        acc[above, lo] = part[lo]
        part = acc[below] + project(below, 1)
        rs_send[3] = part[lo].astype(BF)
        rs.append(reduce_send(3, rs_fin.at[1], down))
        acc[below, hi] = part[hi]
        acc[ty] = (acc[ty] + project(ty, 1)).astype(BF).astype(F32)

    product_back(0)
    send_back(2)
    product_back(1)
    with mark("t1wait"):
        wait_bytes(tap1.at[pl.ds(0, nz - 1)], ts.at[1])
    tap2[e_me] = jnp.sum(tap1[...], axis=0)
    for k in range(1, group_n):
        to = peer_e(lax.rem(e_me + k, group_n))
        start(tap2.at[e_me], tap2.at[e_me], ts.at[2], ts.at[3], to)
    send_back(3)
    with mark("rsmid"):
        rs[0].wait_recv()
        rs_send[4] = (acc[above, lo] + rs_mid[0].astype(F32)).astype(BF)
        rs.append(reduce_send(4, rs_fin.at[2], up))
        rs[1].wait_recv()
        rs_send[5] = (acc[below, hi] + rs_mid[1].astype(F32)).astype(BF)
        rs.append(reduce_send(5, rs_fin.at[3], down))

    leaving = []

    def leave(src, dst):
        copy = pltpu.make_async_copy(src, dst, out_sem.at[len(leaving)])
        copy.start()
        leaving.append(copy)

    def loader_rows(u):
        h = u % HALVES
        with mark(f"bwait{u}"):
            wait_bytes(rbuf2.at[u, pl.ds(0, n - 1)], br.at[u])
        home = mm(hmat[...], rbuf2[u].reshape(2 * length, uw))
        for p in range(2):
            part = home[p * length : (p + 1) * length]
            at = slice(h * hw + p * uw, h * hw + (p + 1) * uw)
            if u < HALVES:
                qg_o[:, at] = part.astype(BF)
            else:
                kg_o[:, at] = (part * vv[:, at].astype(F32)).astype(BF)
        half_at = pl.ds(h * hw, hw)
        held, out = (qg_o, qg_h) if u < HALVES else (kg_o, kg_h)
        leave(held.at[:, half_at], out.at[:, half_at])
        if u >= HALVES:
            for p in range(2):
                part = home[p * length : (p + 1) * length]
                at = slice(h * hw + p * uw, h * hw + (p + 1) * uw)
                vg_o[:, at] = (part * kv[:, at].astype(F32)).astype(BF)
            leave(vg_o.at[:, half_at], vg_h.at[:, half_at])

    loader_rows(0)
    with mark("t2wait"):
        wait_bytes(tap2.at[pl.ds(0, group_n - 1)], ts.at[3])
    summed = tap2[0]
    for i in range(1, group_n):
        summed = summed + tap2[i]
    scale = 1.0 / math.sqrt(float(ndp * total))
    mirror = ones_where(lane == taps - 1 - row)
    fg_o[cz] = scale * jnp.dot(
        summed, mirror, precision=lax.Precision.HIGHEST, preferred_element_type=F32
    )
    for k in range(1, nz):
        to = {CZ: lax.rem(cz + k, nz)}
        start(fg_o.at[cz], fg_o.at[cz], ts.at[4], ts.at[5], to)
    loader_rows(1)
    loader_rows(2)
    with mark("rswait"):
        for copy in rs[2:]:
            copy.wait_recv()
    for rows_of, one, two in ((lo, 1, 2), (hi, 0, 3)):
        summed = acc[ty, rows_of] + rs_fin[one].astype(F32) + rs_fin[two].astype(F32)
        mixed_o[rows_of] = summed.astype(BF)
    leave(mixed_o, mixed_h)
    loader_rows(3)
    with mark("t3wait"):
        wait_bytes(fg_o.at[pl.ds(0, nz - 1)], ts.at[5])
    leave(fg_o, fg_h)

    with mark("drain"):
        for copy in ag + rs + prod_halo + back_halo:
            copy.wait_send()
        wait_bytes(tap1.at[pl.ds(0, nz - 1)], ts.at[0])
        wait_bytes(tap2.at[pl.ds(0, group_n - 1)], ts.at[2])
        wait_bytes(fg_o.at[pl.ds(0, nz - 1)], ts.at[4])
        wait_bytes(sbuf.at[:, pl.ds(0, n - 1)], fs)
        wait_bytes(sbuf2.at[:, pl.ds(0, n - 1)], bs)
        for copy in leaving:
            copy.wait()


def hand_over(*refs):
    count = (len(refs) - 2) // 3
    srcs, dsts, held = refs[:count], refs[count : 2 * count], refs[2 * count : 3 * count]
    sem_in, sem_out = refs[3 * count :]
    ins, outs = [], []
    for a, b, c in zip(srcs, held, dsts, strict=True):
        pieces = 1
        rows = a.shape[0] // pieces
        for p in range(pieces):
            at, i = pl.ds(p * rows, rows), len(ins)
            ins.append(pltpu.make_async_copy(a.at[at], b.at[at], sem_in.at[i]))
            outs.append(pltpu.make_async_copy(b.at[at], c.at[at], sem_out.at[i]))
    for copy in ins:
        copy.start()
    for arrive, leave in zip(ins, outs, strict=True):
        arrive.wait()
        leave.start()
    for copy in outs:
        copy.wait()


def build(mesh, nx, nz):
    ndp, ny = mesh.shape["dp"], mesh.shape["tensor"]
    n = nx * nz
    finer = Mesh(mesh.devices.reshape(ndp, nx, nz, ny), (DP, CX, CZ, TP))

    def per_device(query, key, value, filters, weight, lengths, plan, out_grad):
        length, width = query.shape[1:]
        groups, taps = filters.shape
        cfg = dict(
            n=n, nx=nx, nz=nz, ny=ny, ndp=ndp, length=length, width=width, taps=taps,
            docs=lengths.shape[1], groups=groups,
        )
        hw, blocks, psz = width // HALVES, length // taps, length // n
        uw = hw // 2
        hbm = pl.BlockSpec(memory_space=pl.ANY)
        dma = pltpu.SemaphoreType.DMA
        row = jax.ShapeDtypeStruct((length, width), BF)
        e = ndp * nx
        assert groups == nz * 8
        outs = pl.pallas_call(
            functools.partial(layer_kernel, cfg),
            name="layer",
            out_shape=[row, row, row, row, jax.ShapeDtypeStruct((nz, 8, taps), F32)],
            in_specs=[hbm] * 8,
            out_specs=[hbm] * 5,
            scratch_shapes=[
                pltpu.SMEM(plan.shape, I32),
                pltpu.SMEM(lengths.shape, I32),
                pltpu.VMEM(plan.shape, I32),
                pltpu.VMEM(filters.shape, BF),
                *[pltpu.VMEM((length, width), BF)] * 4,
                pltpu.VMEM((nz, 8, taps), F32),
                *[pltpu.VMEM((HALVES, 2 * length, uw), BF)] * 2,
                pltpu.VMEM((length, width), BF),
                pltpu.VMEM((length, width), BF),
                pltpu.VMEM(weight.shape, BF),
                pltpu.VMEM((ny, length, width), BF),
                *[pltpu.VMEM((2 * length, 2 * length), BF)] * 4,
                *[pltpu.VMEM((UNITS, n, 2 * psz, uw), BF)] * 4,
                pltpu.VMEM((2 * HALVES, length, uw), BF),
                *[pltpu.VMEM((HALVES, length + taps, hw), BF)] * 2,
                pltpu.VMEM((UNITS, 2 * length, uw), BF),
                pltpu.VMEM((length, width), BF),
                *[pltpu.VMEM((2 * HALVES, length, uw), F32)] * 2,
                pltpu.VMEM((ny, length, width), F32),
                *[pltpu.VMEM((blocks, groups * taps, 2 * taps), BF)] * 2,
                *[pltpu.VMEM((blocks, taps, 2 * taps), F32)] * 3,
                *[pltpu.VMEM((k, length // 2, width), BF) for k in (6, 2, 4)],
                *[pltpu.VMEM((nz, 8, taps), F32)] * 2,
                pltpu.VMEM((e, 8, taps), F32),
                pltpu.VMEM((2, groups, taps), F32),
                dma((4,)), dma((8,)), dma((8,)),
                dma, dma((UNITS,)),
                dma((6,)), dma((6,)),
                *[dma((HALVES,))] * 4,
                dma, dma((UNITS,)),
                dma((6,)), dma((6,)),
                dma((6,)),
            ],
            compiler_params=pltpu.CompilerParams(
                collective_id=0, has_side_effects=True, vmem_limit_bytes=67043328
            ),
        )(plan, lengths, filters, query[0], key[0], value[0], out_grad[0], weight)
        moved = pl.pallas_call(
            hand_over,
            name="results",
            out_shape=[jax.ShapeDtypeStruct(o.shape, o.dtype) for o in outs],
            in_specs=[hbm] * 5,
            out_specs=[hbm] * 5,
            scratch_shapes=[pltpu.VMEM(o.shape, o.dtype) for o in outs] + [dma((5,)), dma((5,))],
        )(*outs)
        mixed, qg, kg, vg, fg = moved
        return mixed[None], qg[None], kg[None], vg[None], fg.reshape(groups, taps)

    rows = P(DP, CONTEXT, TP)
    split = P(TP, None)
    return jax.shard_map(
        per_device,
        mesh=finer,
        in_specs=(rows, rows, rows, split, split, P(DP, None), P(DP, None), rows),
        out_specs=(rows, rows, rows, rows, split),
        check_vma=False,
    )


def solution(mesh):
    return build(mesh, 4, mesh.shape["context"] // 4)
```
